32 devices in a mesh: tm: 4 (over x, core), height: 8 (over z, y).
Axes of the slice: x: 2, y: 2, z: 4, core: 2. Of those that a mesh axis runs over, the one named last changes fastest.
Arguments:
- queries: bfloat16 [16, 64, 4, 1536], P('tm', 'height'), may hold values from -6 to 6
- key_tokens: bfloat16 [16, 64, 4, 1536], P('tm', 'height'), may hold values from -6 to 6
- value_tokens: bfloat16 [16, 64, 4, 1536], P('tm', 'height'), may hold values from -6 to 6
- out_weight: bfloat16 [1536, 3072], P('height'), may hold values from -0.15625 to 0.15625
- out_grad: bfloat16 [16, 64, 4, 3072], P('tm', 'height'), may hold values from -6 to 6
- window_reach: int32 [4, 8, 2], replicated, may hold values from 0 to 2, as said below
- tile_valid: int32 [4, 8], replicated, may hold values 0 or 1
Outputs:
- attn_out: bfloat16 [16, 64, 4, 3072], P('tm', 'height')
- grad_query: bfloat16 [16, 64, 4, 1536], P('tm', 'height')
- grad_key: bfloat16 [16, 64, 4, 1536], P('tm', 'height')
- grad_value: bfloat16 [16, 64, 4, 1536], P('tm', 'height')
- grad_weight: float32 [1536, 3072], P('height', 'tm')
The draws below stay inside these ranges and needn't reach their ends.
Inputs may be any that keep to these rules, and one draw needn't show every extreme that they name: `window_reach`: entry 0 is a tile's reach in frames and entry 1 its reach in rows; some tile reaches 2 in both.
All inputs are finite; a program needn't handle non-finite values.
Results may differ from the reference program's by a relative error of at most 0.014.
Values may be sent and summed in bfloat16 or wider, within the bound.
A program may use at most 128 MiB of HBM per device.

```python
import math
import jax
import jax.numpy as jnp
from jax import lax

D = 3072
HEAD_DIM = 128
HEADS = 12
HD = 1536
TF = 4
TR = 8
COLS = 4
HALO = 2
TOK = 128
TILES_T = 4
TILES_H = 8
FRAMES = 16
ROWS = 64


def drawn_pair(key):
    base_key = jax.random.fold_in(key, 7)
    subkeys = jax.random.split(base_key, 2)
    shape = (FRAMES, ROWS, COLS // 2, 2, HD)
    first = jax.random.truncated_normal(subkeys[0], -6.0, 6.0, shape, jnp.float32)
    second = jax.random.truncated_normal(subkeys[1], -6.0, 6.0, shape, jnp.float32)
    return (first.reshape(FRAMES, ROWS, COLS, HD), second.reshape(FRAMES, ROWS, COLS, HD))


def draw_queries(key, part):
    return drawn_pair(key)[0].astype(jnp.bfloat16)


def draw_key_tokens(key, part):
    return drawn_pair(key)[1].astype(jnp.bfloat16)


def draw_window_reach(key, part):
    subkeys = jax.random.split(jax.random.fold_in(key, 11), 4)
    reach_frame = jax.random.randint(subkeys[0], (TILES_T, TILES_H, 1), 0, HALO + 1, dtype=jnp.int32)
    reach_row = jax.random.randint(subkeys[1], (TILES_T, TILES_H, 1), 0, HALO + 1, dtype=jnp.int32)
    chosen_frame = jax.random.randint(subkeys[2], (), 0, TILES_T, dtype=jnp.int32)
    chosen_row = jax.random.randint(subkeys[3], (), 0, TILES_H, dtype=jnp.int32)
    marked = (jnp.arange(TILES_T, dtype=jnp.int32)[:, None] == chosen_frame) & (jnp.arange(TILES_H, dtype=jnp.int32)[None, :] == chosen_row)
    joined = jnp.concatenate([reach_frame, reach_row], axis=2)
    return jnp.where(marked[:, :, None], jnp.int32(HALO), joined).astype(jnp.int32)


def with_ends(array, rng, low, high):
    extent = array.shape
    spot = [jax.random.randint(jax.random.fold_in(rng, axis), (), 0, extent[axis]) for axis in range(len(extent))]
    array = array.at[tuple(spot)].set(low)
    longest = extent.index(max(extent))
    spot[longest] = (spot[longest] + 1) % extent[longest]
    return array.at[tuple(spot)].set(high)


def spiked(array, key, source, target, blocks, factor):
    owner, partner = [(jnp.arange(array.shape[dim]) // (array.shape[dim] // blocks)).reshape([-1 if axis == dim else 1 for axis in range(array.ndim)]) for dim in (source, target)]
    chosen = jax.random.permutation(key, blocks)[partner]
    strong = (owner == chosen) | (owner == (partner + blocks // 2) % blocks)
    return jnp.where(strong, factor * array, array)


def steps_of(own_key, dims, pieces, least, top_value):
    factor_of = 1.0
    for dim, parts in pieces:
        draws = jax.random.uniform(jax.random.fold_in(jax.random.fold_in(own_key, 6), dim), (parts,), jnp.float32, least / len(pieces), top_value / len(pieces))
        factor_of = factor_of * jnp.repeat(jnp.exp(draws), dims[dim] // parts).reshape((-1,) + (1,) * (len(dims) - 1 - dim))
    return factor_of


def centred(key, dims, width, most, cuts=(), kind=jnp.bfloat16):
    array = width * jax.random.normal(key, dims, jnp.float32)
    if cuts:
        array = array * steps_of(key, dims, cuts, -0.22, 0.18)
    return jnp.clip(array, -most, most).astype(kind)


def bell_draw_with(key, shape, spread, limit, cuts, heavy, kind=jnp.bfloat16):
    values = spread * jax.random.normal(key, shape, jnp.float32)
    if cuts:
        values = values * steps_of(key, shape, cuts, -0.22, 0.18)
    return jnp.clip(spiked(values, jax.random.fold_in(key, 3), *heavy), -limit, limit).astype(kind)


def setup_inputs(seed: int = 0) -> dict:
    seeds = jax.random.split(jax.random.key(seed), 8)
    queries = draw_queries(jax.random.fold_in(seeds[7], 71), 0)
    key_tokens = draw_key_tokens(jax.random.fold_in(seeds[7], 71), 0)
    value_tokens = centred(seeds[2], (FRAMES, ROWS, COLS, HD), 1.0, 6.0, ((0, 4), (1, 8)))
    out_weight = centred(seeds[3], (HD, D), HD ** -0.5, 0.15625, ((0, 8),))
    out_grad = bell_draw_with(seeds[4], (FRAMES, ROWS, COLS, D), 1.0, 6.0, ((0, 4), (1, 8)), (0, 3, 4, 2.0))
    window_reach = draw_window_reach(jax.random.fold_in(seeds[7], 71), 0)
    tile_valid = with_ends((jax.random.randint(seeds[6], (TILES_T, TILES_H), 0, 4) < 3).astype(jnp.int32), jax.random.fold_in(seeds[6], 1), 0, 1)
    return {"queries": queries, "key_tokens": key_tokens, "value_tokens": value_tokens, "out_weight": out_weight, "out_grad": out_grad, "window_reach": window_reach, "tile_valid": tile_valid}


def tile_allowed(window_reach, tile_valid, frame_tile, row_tile):
    ext_frames = TF + 2 * HALO
    ext_rows = TR + 2 * HALO
    frame_pos = jnp.arange(ext_frames, dtype=jnp.int32)
    row_pos = jnp.arange(ext_rows, dtype=jnp.int32)
    global_frame = frame_tile * TF - HALO + frame_pos
    global_row = row_tile * TR - HALO + row_pos
    reach_frame = window_reach[frame_tile, row_tile, 0]
    reach_row = window_reach[frame_tile, row_tile, 1]
    own_frame = (frame_pos >= HALO) & (frame_pos < HALO + TF)
    own_row = (row_pos >= HALO) & (row_pos < HALO + TR)
    near_frame = (frame_pos >= HALO - reach_frame) & (frame_pos < HALO + TF + reach_frame)
    near_frame = near_frame & (global_frame >= 0) & (global_frame < FRAMES)
    near_row = (row_pos >= HALO - reach_row) & (row_pos < HALO + TR + reach_row)
    near_row = near_row & (global_row >= 0) & (global_row < ROWS)
    key_frame_tile = jnp.clip(jnp.floor_divide(global_frame, TF), 0, TILES_T - 1).astype(jnp.int32)
    key_row_tile = jnp.clip(jnp.floor_divide(global_row, TR), 0, TILES_H - 1).astype(jnp.int32)
    valid = tile_valid[key_frame_tile[:, None], key_row_tile[None, :]] == 1
    allowed = own_frame[:, None] & own_row[None, :] | near_frame[:, None] & near_row[None, :] & valid
    return jnp.broadcast_to(allowed[:, :, None], (ext_frames, ext_rows, COLS)).reshape(-1)

def reference(queries, key_tokens, value_tokens, out_weight, out_grad, window_reach, tile_valid):
    ext_frames = TF + 2 * HALO
    ext_rows = TR + 2 * HALO
    ext_count = ext_frames * ext_rows * COLS
    score_scale = 1.0 / math.sqrt(HEAD_DIM)
    d_mixed_all = jnp.dot(out_grad.reshape(-1, D), out_weight.T, preferred_element_type=jnp.float32)
    d_mixed_all = d_mixed_all.astype(jnp.bfloat16).reshape(FRAMES, ROWS, COLS, HD)
    padding = ((HALO, HALO), (HALO, HALO), (0, 0), (0, 0))
    padded_keys = jnp.pad(key_tokens, padding)
    padded_values = jnp.pad(value_tokens, padding)
    zero_grads = jnp.zeros((FRAMES + 2 * HALO, ROWS + 2 * HALO, COLS, HD), jnp.float32)
    zero_weight = jnp.zeros((HD, D), jnp.float32)

    def one_tile(carry, tile_index):
        key_acc, value_acc, weight_acc = carry
        frame_tile = (tile_index // TILES_H).astype(jnp.int32)
        row_tile = (tile_index % TILES_H).astype(jnp.int32)
        start_frame = (frame_tile * TF).astype(jnp.int32)
        start_row = (row_tile * TR).astype(jnp.int32)
        zero_index = jnp.zeros((), jnp.int32)
        corner = (start_frame, start_row, zero_index, zero_index)
        q_tile = lax.dynamic_slice(queries, corner, (TF, TR, COLS, HD)).reshape(TOK, HEADS, HEAD_DIM)
        dm_tile = lax.dynamic_slice(d_mixed_all, corner, (TF, TR, COLS, HD)).reshape(TOK, HEADS, HEAD_DIM)
        grad_tile = lax.dynamic_slice(out_grad, corner, (TF, TR, COLS, D)).reshape(TOK, D)
        k_ext = lax.dynamic_slice(padded_keys, corner, (ext_frames, ext_rows, COLS, HD)).reshape(ext_count, HEADS, HEAD_DIM)
        v_ext = lax.dynamic_slice(padded_values, corner, (ext_frames, ext_rows, COLS, HD)).reshape(ext_count, HEADS, HEAD_DIM)
        allowed = tile_allowed(window_reach, tile_valid, frame_tile, row_tile)
        q32 = q_tile.astype(jnp.float32)
        k32 = k_ext.astype(jnp.float32)
        v32 = v_ext.astype(jnp.float32)
        dm32 = dm_tile.astype(jnp.float32)
        scores = jnp.einsum('qhd,khd->hqk', q32, k32) * score_scale
        scores = jnp.where(allowed[None, None, :], scores, -1e+30)
        row_max = lax.optimization_barrier(jnp.max(scores, axis=-1, keepdims=True))
        expo = jnp.exp(scores - row_max)
        prob = expo / lax.optimization_barrier(jnp.sum(expo, axis=-1, keepdims=True))
        probs = prob.astype(jnp.bfloat16)
        probs32 = probs.astype(jnp.float32)
        mixed = jnp.einsum('hqk,khd->qhd', probs32, v32).astype(jnp.bfloat16)
        d_probs = jnp.einsum('qhd,khd->hqk', dm32, v32)
        inner = lax.optimization_barrier(jnp.sum(prob * d_probs, axis=-1, keepdims=True))
        d_scores = (prob * (d_probs - inner) * score_scale).astype(jnp.bfloat16).astype(jnp.float32)
        d_query = jnp.einsum('hqk,khd->qhd', d_scores, k32).astype(jnp.bfloat16)
        d_key = jnp.einsum('hqk,qhd->khd', d_scores, q32).reshape(ext_frames, ext_rows, COLS, HD)
        d_value = jnp.einsum('hqk,qhd->khd', probs32, dm32).reshape(ext_frames, ext_rows, COLS, HD)
        key_acc = lax.dynamic_update_slice(key_acc, lax.dynamic_slice(key_acc, corner, (ext_frames, ext_rows, COLS, HD)) + d_key, corner)
        value_acc = lax.dynamic_update_slice(value_acc, lax.dynamic_slice(value_acc, corner, (ext_frames, ext_rows, COLS, HD)) + d_value, corner)
        mixed_rows = mixed.reshape(TOK, HD)
        term = jnp.dot(mixed_rows.T, grad_tile, preferred_element_type=jnp.float32).astype(jnp.bfloat16)
        term = lax.optimization_barrier(term).astype(jnp.float32)
        return ((key_acc, value_acc, weight_acc + term), (mixed, d_query))
    tile_ids = jnp.arange(TILES_T * TILES_H, dtype=jnp.int32)
    carry, stacked = lax.scan(one_tile, (zero_grads, zero_grads, zero_weight), tile_ids)
    key_acc, value_acc, grad_weight = carry
    mixed_tiles, dq_tiles = stacked

    def untile(tiles):
        shaped = tiles.reshape(TILES_T, TILES_H, TF, TR, COLS, HD)
        return shaped.transpose(0, 2, 1, 3, 4, 5).reshape(FRAMES, ROWS, COLS, HD)
    mixed_all = untile(mixed_tiles)
    grad_query = untile(dq_tiles)
    attn_out = jnp.dot(mixed_all.reshape(-1, HD), out_weight, preferred_element_type=jnp.float32)
    attn_out = attn_out.astype(jnp.bfloat16).reshape(FRAMES, ROWS, COLS, D)
    grad_key = key_acc[HALO:HALO + FRAMES, HALO:HALO + ROWS].astype(jnp.bfloat16)
    grad_value = value_acc[HALO:HALO + FRAMES, HALO:HALO + ROWS].astype(jnp.bfloat16)
    return (attn_out, grad_query, grad_key, grad_value, grad_weight)
```

```python
import functools
import math

import jax
import jax.numpy as jnp
import numpy as np
from jax import lax
from jax.experimental import pallas as pl
from jax.experimental.pallas import tpu as pltpu
from jax.sharding import PartitionSpec as P

HEAD_DIM = 128
HALO = 2
MESH = pl.DeviceIdType.MESH
F32 = jnp.float32
BF16 = jnp.bfloat16
SIDES = ((-1, 0), (1, 0), (0, -1), (0, 1), (-1, -1), (-1, 1), (1, -1), (1, 1))


def piece_sizes(frames, rows, columns):
    sizes = []
    for df, dr in SIDES:
        sizes.append((HALO if df else frames) * (HALO if dr else rows) * columns)
    return sizes


def key_table(frames, rows, columns, sides=SIDES):
    table = []
    for piece, (df, dr) in enumerate(((0, 0),) + sides):
        for f in range(HALO) if df else range(frames):
            for r in range(HALO) if dr else range(rows):
                fd = 0 if df == 0 else (HALO - f if df < 0 else f + 1)
                rd = 0 if dr == 0 else (HALO - r if dr < 0 else r + 1)
                table += [(piece, fd, rd)] * columns
    return np.ascontiguousarray(np.array(table, np.int32).T)


def piece_rows(df, dr, frames, rows, columns):
    fs = range(frames) if df == 0 else (range(frames - HALO, frames) if df < 0 else range(HALO))
    if dr == 0:
        return [(fs[0] * rows * columns, len(fs) * rows * columns)]
    first = (rows - HALO) if dr < 0 else 0
    return [((f * rows + first) * columns, HALO * columns) for f in fs]


def kernel(
    dims,
    q_ref, k_ref, v_ref, table_ref, reach_ref, valid_ref, w_hbm, og_hbm,
    attn_ref, dq_ref, dk_ref, dv_ref, gw_ref,
    wfull, ogown, ogcols, kvsend, kvext, gsend, grecv, prob, dmixed, mixed, mixall, acc, gpart, bias_ref, gwsend, gwrecv,
    local_sem, halo_s, halo_r, grad_s, grad_r, mix_s, mix_r,
    wr_s, wr_r, wl_s, wl_r, wc_s, wc_r, og_s, og_r, gw_s, gw_r,
):
    nt, nh, frames, rows, columns = dims
    t, h = lax.axis_index("tm"), lax.axis_index("height")
    tokens, width = q_ref.shape
    model = og_hbm.shape[1]
    share = w_hbm.shape[0]
    heads = width // HEAD_DIM
    half = model // 2
    window = gpart.shape[1]
    span_cols = model // nt
    scale = 1.0 / math.sqrt(HEAD_DIM)
    sizes = piece_sizes(frames, rows, columns)
    starts = [sum(sizes[:i]) for i in range(8)]

    def place(df, dr):
        return (lax.rem(t + nt + df, nt), lax.rem(h + nh + dr, nh))

    def exists(df, dr):
        a, b = t + df, h + dr
        return (a >= 0) & (a < nt) & (b >= 0) & (b < nh)

    def exchange(copies, sign, action):
        for (df, dr), copy in zip(SIDES, copies):
            if action == "start":
                pl.when(exists(sign * df, sign * dr))(copy.start)
            else:
                pl.when(exists(sign * df, sign * dr))(copy.wait_send)
                pl.when(exists(-sign * df, -sign * dr))(copy.wait_recv)

    def remote(src, dst, ssem, rsem, where):
        return pltpu.make_async_remote_copy(
            src_ref=src, dst_ref=dst, send_sem=ssem, recv_sem=rsem,
            device_id=where, device_id_type=MESH,
        )

    def wrow(j, lo=0, size=None):
        return pl.ds(pl.multiple_of(j * share + lo, 16), share if size is None else size)

    def orow(j, lo=0, size=None):
        return pl.ds(pl.multiple_of(j * tokens + lo, 16), tokens if size is None else size)

    own_w = pltpu.make_async_copy(w_hbm, wfull.at[wrow(h), :], local_sem.at[0])
    own_og = pltpu.make_async_copy(og_hbm, ogown, local_sem.at[1])
    own_w.start()
    own_og.start()

    barrier = pltpu.get_barrier_semaphore()
    greeted = 0
    for i in range(1, nh):
        pl.semaphore_signal(barrier, inc=1, device_id=(t, lax.rem(h + i, nh)), device_id_type=MESH)
        greeted += 1
    for i in range(1, nt):
        pl.semaphore_signal(barrier, inc=1, device_id=(lax.rem(t + i, nt), h), device_id_type=MESH)
        greeted += 1
    for df, dr in SIDES:
        if df and dr:
            pl.semaphore_signal(barrier, inc=1, device_id=place(df, dr), device_id_type=MESH)
            greeted += 1

    piece = table_ref[0:1, :]
    hit = jnp.ones_like(piece)
    for s, (df, dr) in enumerate(SIDES):
        a, b = place(df, dr)
        here = jnp.where(exists(df, dr), valid_ref[a, b], 0)
        hit = jnp.where(piece == s + 1, here, hit)
    near = (table_ref[1:2, :] <= reach_ref[t, h, 0]) & (table_ref[2:3, :] <= reach_ref[t, h, 1])
    bias_ref[...] = jnp.where((piece == 0) | (near & (hit == 1)), 0.0, -1e30)

    for i, ref in enumerate((k_ref, v_ref)):
        x = ref[...]
        kvext[i, 0:tokens, :] = x
        x = x.astype(F32)
        for s, (df, dr) in enumerate(SIDES):
            parts = [x[a : a + n] for a, n in piece_rows(df, dr, frames, rows, columns)]
            y = parts[0] if len(parts) == 1 else jnp.concatenate(parts, axis=0)
            kvsend[i, starts[s] : starts[s] + sizes[s], :] = y.astype(BF16)

    for s, (df, dr) in enumerate(SIDES):

        @pl.when(jnp.logical_not(exists(df, dr)))
        def _():
            rs = pl.ds(tokens + starts[s], sizes[s])
            kvext[:, rs, :] = jnp.zeros((2, sizes[s], width), BF16)

    par = lax.rem(h, 2)
    pos = (1 - par) * (h // 2) + par * (nh - 1 - h // 2)

    def at(p):
        p = lax.rem(p + nh, nh)
        far = p // (nh // 2)
        return (1 - far) * (2 * p) + far * (2 * (nh - 1 - p) + 1)

    right, left = (t, at(pos + 1)), (t, at(pos - 1))
    steps = nh // 2
    core = lax.rem(t, 2)
    partner = (t + 1 - 2 * core, h)
    mine = pl.ds(pl.multiple_of(core * half, 128), half)

    def span(step, size, side):
        if step < steps - 1:
            return 0, size
        return (0 if side == 0 else size // 2), size // 2

    def ring_sends(step, buf, rowfn, size, cols, sems):
        out = []
        for side, (target, sign) in enumerate(((right, -1), (left, 1))):
            lo, n = span(step, size, side)
            ref = buf.at[rowfn(at(pos + sign * step), lo, n), cols]
            ssem, rsem = sems[2 * side], sems[2 * side + 1]
            copy = remote(ref, ref, ssem.at[step], rsem.at[step], target)
            copy.start()
            out.append(copy)
        return out

    wsems = (wr_s, wr_r, wl_s, wl_r)
    def w_sends(step):
        return ring_sends(step, wfull, wrow, share, mine, wsems)

    def gw_sends(step):
        out = []
        for side, (target, sign) in enumerate(((right, 1), (left, -1))):
            base = at(pos + sign * (steps - step)) * share
            cut = share // 2
            for part in range(2):
                if step == 0 and part != side:
                    continue
                rs = slice(part * cut, (part + 1) * cut)
                total = gpart[pl.ds(pl.multiple_of(base + part * cut, 16), cut), :]
                if step > 1 or (step == 1 and part == side):
                    total += gwrecv[side, step - 1, rs, :].astype(F32)
                gwsend[side, step, rs, :] = total.astype(BF16)
            rs = pl.ds(side * cut, cut) if step == 0 else pl.ds(0, share)
            i = side * steps + step
            copy = remote(
                gwsend.at[side, step, rs, :], gwrecv.at[side, step, rs, :],
                gw_s.at[i], gw_r.at[i], target,
            )
            copy.start()
            out.append(copy)
        return out

    def cols_start(j):
        block = jnp.minimum((j * span_cols) // 128, (model - window) // 128)
        return pl.multiple_of(block * 128, 128)

    def share_sends(step):
        out = []
        for side, sign in enumerate((-1, 1)):
            lo, n = span(step, share, side)
            ref = wfull.at[wrow(at(pos + sign * (step + 1)), lo, n), mine]
            i = 2 * step + side
            out.append(remote(ref, ref, wc_s.at[i], wc_r.at[i], partner))
        for copy in out:
            copy.start()
        return out

    own_w.wait()
    own_og.wait()
    pl.semaphore_wait(barrier, greeted)
    halos = []
    for s, (df, dr) in enumerate(SIDES):
        copy = remote(
            kvsend.at[:, pl.ds(starts[s], sizes[s]), :],
            kvext.at[:, pl.ds(tokens + starts[s], sizes[s]), :],
            halo_s.at[s], halo_r.at[s], place(-df, -dr),
        )
        halos.append(copy)
    exchange(halos, -1, "start")
    live = w_sends(0)
    ogcols[orow(t), :] = ogown[:, pl.ds(cols_start(t), window)]
    gathers = []
    for i in range(1, nt):
        j = lax.rem(t + i, nt)
        copy = remote(
            ogown.at[:, pl.ds(cols_start(j), window)], ogcols.at[orow(t), :],
            og_s.at[i - 1], og_r.at[i - 1], (j, h),
        )
        copy.start()
        gathers.append(copy)
    shared = []

    def w_step(step):
        for copy in live:
            copy.wait()
        live.clear()
        if step < steps - 1:
            live.extend(w_sends(step + 1))
        shared.extend(share_sends(step))

    for step in range(2):
        w_step(step)
    exchange(halos, -1, "wait")

    group = 3 if heads % 3 == 0 else 1

    def cols_of(c):
        return pl.ds(pl.multiple_of(c * HEAD_DIM, HEAD_DIM), HEAD_DIM)

    def nt_dot(a, b):
        return lax.dot_general(a, b, (((1,), (1,)), ((), ())), preferred_element_type=F32)

    def tn_dot(a, b):
        return lax.dot_general(a, b, (((0,), (0,)), ((), ())), preferred_element_type=F32)

    def nn_dot(a, b):
        return lax.dot_general(a, b, (((1,), (0,)), ((), ())), preferred_element_type=F32)

    def forward(g, carry):
        for j in range(group):
            c = g * group + j
            cs = cols_of(c)
            scores = nt_dot(q_ref[:, cs], kvext[0, :, cs]) * scale + bias_ref[...]
            e = jnp.exp(scores - jnp.max(scores, axis=-1, keepdims=True))
            p = e / jnp.sum(e, axis=-1, keepdims=True)
            prob[c] = p
            mixed[:, cs] = nn_dot(p.astype(BF16), kvext[1, :, cs]).astype(BF16)
        return carry

    lax.fori_loop(0, heads // group, forward, 0)

    mixall[orow(t), :] = mixed[...]
    for i in range(1, nt):
        copy = remote(
            mixed, mixall.at[orow(t), :], mix_s.at[i - 1], mix_r.at[i - 1],
            (lax.rem(t + i, nt), h),
        )
        copy.start()
        gathers.append(copy)

    def gw_step(step):
        for copy in live:
            copy.wait()
        live.clear()
        if step < steps:
            live.extend(gw_sends(step))

    for step in range(2, steps):
        w_step(step)

    for copy in gathers:
        copy.wait()

    def weight(i, carry):
        cs = pl.ds(pl.multiple_of(i * 256, 256), 256)
        gpart[cs, :] = tn_dot(mixall[:, cs], ogcols[...])
        return carry

    lax.fori_loop(0, width // 256, weight, 0)
    gw_step(0)
    for copy in shared:
        copy.wait()

    def project(i, carry):
        r = pl.ds(pl.multiple_of(i * 256, 256), 256)
        dmixed[:, r] = nt_dot(ogown[...], wfull[r, :]).astype(BF16)
        return carry

    lax.fori_loop(0, width // 256, project, 0)

    gw_step(1)

    def backward(g, carry):
        for j in range(group):
            c = g * group + j
            cs = cols_of(c)
            p = prob[c]
            dm = dmixed[:, cs]
            dp = nt_dot(dm, kvext[1, :, cs])
            inner = jnp.sum(p * dp, axis=-1, keepdims=True)
            ds = (p * (dp - inner) * scale).astype(BF16)
            dq_ref[:, cs] = nn_dot(ds, kvext[0, :, cs]).astype(BF16)
            dk = tn_dot(ds, q_ref[:, cs])
            dv = tn_dot(p.astype(BF16), dm)
            acc[0, :, cs] = dk[:tokens]
            acc[1, :, cs] = dv[:tokens]
            gsend[0, :, cs] = dk[tokens:].astype(BF16)
            gsend[1, :, cs] = dv[tokens:].astype(BF16)
        return carry

    lax.fori_loop(0, heads // group, backward, 0)

    grads = []
    for s, (df, dr) in enumerate(SIDES):
        rs = pl.ds(starts[s], sizes[s])
        copy = remote(
            gsend.at[:, rs, :], grecv.at[:, rs, :], grad_s.at[s], grad_r.at[s], place(df, dr)
        )
        grads.append(copy)
    exchange(grads, 1, "start")
    gw_step(2)

    def attn(i, carry):
        cs = pl.ds(pl.multiple_of(i * 256, 256), 256)
        attn_ref[:, cs] = nn_dot(mixed[...], wfull[:, cs]).astype(BF16)
        return carry

    lax.fori_loop(0, model // 256, attn, 0)
    gw_step(3)

    exchange(grads, 1, "wait")
    for i, ref in enumerate((dk_ref, dv_ref)):
        for s, (df, dr) in enumerate(SIDES):

            @pl.when(exists(-df, -dr))
            def _():
                y = grecv[i, starts[s] : starts[s] + sizes[s], :].astype(F32)
                first = 0
                for a, n in piece_rows(df, dr, frames, rows, columns):
                    acc[i, a : a + n, :] += y[first : first + n]
                    first += n

        ref[...] = acc[i].astype(BF16)

    for step in range(4, steps + 1):
        gw_step(step)
    gw_ref[...] = (
        gpart[wrow(h), :]
        + gwrecv[0, steps - 1].astype(F32)
        + gwrecv[1, steps - 1].astype(F32)
    )


def shards(nt, nh, queries, key_tokens, value_tokens, out_weight, out_grad, window_reach, tile_valid):
    frames, rows, columns, width = queries.shape
    model = out_grad.shape[3]
    share = out_weight.shape[0]
    tokens = frames * rows * columns
    heads = width // HEAD_DIM
    halo = sum(piece_sizes(frames, rows, columns))
    ext = tokens + halo
    table = key_table(frames, rows, columns)
    narrow = (model // nt) % 128 == 0
    block = model // nt if narrow else 256
    steps = nh // 2
    vmem = pl.BlockSpec(memory_space=pltpu.VMEM)
    smem = pl.BlockSpec(memory_space=pltpu.SMEM)
    hbm = pl.BlockSpec(memory_space=pl.ANY)
    dma = pltpu.SemaphoreType.DMA
    attn, dq, dk, dv, gw = pl.pallas_call(
        functools.partial(kernel, (nt, nh, frames, rows, columns)),
        out_shape=(
            jax.ShapeDtypeStruct((tokens, model), BF16),
            jax.ShapeDtypeStruct((tokens, width), BF16),
            jax.ShapeDtypeStruct((tokens, width), BF16),
            jax.ShapeDtypeStruct((tokens, width), BF16),
            jax.ShapeDtypeStruct((share, block), F32),
        ),
        in_specs=[vmem, vmem, vmem, vmem, smem, smem, hbm, hbm],
        out_specs=[vmem] * 5,
        scratch_shapes=[
            pltpu.VMEM((width, model), BF16),
            pltpu.VMEM((tokens, model), BF16),
            pltpu.VMEM((nt * tokens, block), BF16),
            pltpu.VMEM((2, halo, width), BF16),
            pltpu.VMEM((2, ext, width), BF16),
            pltpu.VMEM((2, halo, width), BF16),
            pltpu.VMEM((2, halo, width), BF16),
            pltpu.VMEM((heads, tokens, ext), F32),
            pltpu.VMEM((tokens, width), BF16),
            pltpu.VMEM((tokens, width), BF16),
            pltpu.VMEM((nt * tokens, width), BF16),
            pltpu.VMEM((2, tokens, width), F32),
            pltpu.VMEM((width, block), F32),
            pltpu.VMEM((1, ext), F32),
            pltpu.VMEM((2, steps, share, block), BF16),
            pltpu.VMEM((2, steps, share, block), BF16),
            dma((2,)), dma((8,)), dma((8,)), dma((8,)), dma((8,)),
            dma((nt - 1,)), dma((nt - 1,)),
            dma((steps,)), dma((steps,)), dma((steps,)), dma((steps,)),
            dma((2 * steps,)), dma((2 * steps,)),
            dma((nt - 1,)), dma((nt - 1,)), dma((2 * steps,)), dma((2 * steps,)),
        ],
        compiler_params=pltpu.CompilerParams(
            collective_id=0, has_side_effects=True, vmem_limit_bytes=56 * 2**20
        ),
    )(
        queries.reshape(tokens, width),
        key_tokens.reshape(tokens, width),
        value_tokens.reshape(tokens, width),
        table,
        window_reach,
        tile_valid,
        out_weight,
        out_grad.reshape(tokens, model),
    )
    if not narrow:
        size = model // nt
        at = lax.axis_index("tm") * size
        first = jnp.minimum(at // 128, (model - block) // 128) * 128
        gw = lax.dynamic_slice_in_dim(gw, at - first, size, axis=1)
    tile = (frames, rows, columns)
    return (
        attn.reshape(*tile, model),
        dq.reshape(*tile, width),
        dk.reshape(*tile, width),
        dv.reshape(*tile, width),
        gw,
    )


ORDER = ((-1, 0), (-1, -1), (-1, 1), (1, 0), (1, -1), (1, 1), (0, -1), (0, 1))


def paired_kernel(
    dims,
    q_hbm, k_hbm, v_hbm, og_hbm, w_hbm, table_ref, reach_ref, valid_ref,
    attn_ref, dq_ref, dk_ref, dv_ref, gw_ref,
    in4, og4, q2, dq2, kvext, rsend, wfull, ogown, og2, ogc, prob, mix, dmx, dms, dmr, attn2, asend,
    acc, ud, gsend, grecv, rrecv, gpart, gws, gwr, bias,
    ld, row_s, row_r, fr_s, fr_r, co_s, co_r, w_s, w_r, sh_s, sh_r, og_s, og_r, mx_s, mx_r,
    mc_s, mc_r, dm_s, dm_r, at_s, at_r, g1_s, g1_r, g2_s, g2_r, gw_s, gw_r,
):
    nt, nh, frames, rows, columns = dims
    t, h = lax.axis_index("tm"), lax.axis_index("height")
    tokens, width = q2.shape
    model = ogown.shape[1]
    share = w_hbm.shape[0]
    half, quarter = model // 2, model // 4
    cut = share // 2
    groups = 4
    gsize = width // groups
    gheads = gsize // HEAD_DIM
    tile = (frames, rows, columns)
    scale = 1.0 / math.sqrt(HEAD_DIM)
    x, core = t // 2, lax.rem(t, 2)
    partner = (t + 1 - 2 * core, h)
    across = (lax.rem(t + 2, nt), h)
    side_rows = HALO * rows * columns
    corner = HALO * HALO * columns
    strip = frames * HALO * columns
    wing = side_rows + 2 * corner
    nwing = 2 * wing
    early, later = tokens, tokens + wing
    up, down = tokens + 2 * wing, tokens + 2 * wing + strip
    before_t, after_t, before_h, after_h = t > 0, t < nt - 1, h > 0, h < nh - 1

    def remote(src, dst, ssem, rsem, where):
        return pltpu.make_async_remote_copy(
            src_ref=src, dst_ref=dst, send_sem=ssem, recv_sem=rsem,
            device_id=where, device_id_type=MESH,
        )

    def gcols(g):
        return pl.ds(pl.multiple_of(g * gsize, 128), gsize)

    par = lax.rem(h, 2)
    pos = (1 - par) * (h // 2) + par * (nh - 1 - h // 2)

    def at(p):
        p = lax.rem(p + nh, nh)
        far = p // (nh // 2)
        return (1 - far) * (2 * p) + far * (2 * (nh - 1 - p) + 1)

    right, left = (t, at(pos + 1)), (t, at(pos - 1))
    mine = pl.ds(pl.multiple_of(core * quarter, 128), quarter)
    other = pl.ds(pl.multiple_of((1 - core) * quarter, 128), quarter)
    xcols = pl.ds(pl.multiple_of(x * half, 128), half)
    ycols = pl.ds(pl.multiple_of((1 - x) * half, 128), half)
    slots = nh - 1

    loads = [
        pltpu.make_async_copy(k_hbm, in4.at[0], ld.at[0]),
        pltpu.make_async_copy(v_hbm, in4.at[1], ld.at[1]),
        pltpu.make_async_copy(og_hbm, og4, ld.at[2]),
        pltpu.make_async_copy(
            w_hbm.at[:, xcols], wfull.at[pl.ds(pl.multiple_of(h * share, 16), share), :], ld.at[3]
        ),
        pltpu.make_async_copy(q_hbm, in4.at[2], ld.at[4]),
    ]
    for copy in loads:
        copy.start()

    barrier = pltpu.get_barrier_semaphore()
    peers = [(lax.rem(t + i, nt), h) for i in range(1, nt)]
    peers += [(t, lax.rem(h + 1, nh)), (t, lax.rem(h + nh - 1, nh)), right, left]
    for peer in peers:
        pl.semaphore_signal(barrier, inc=1, device_id=peer, device_id_type=MESH)

    for i in range(2):
        loads[i].wait()
        y = in4[i].astype(F32).reshape(tokens, width)
        kvext[i, 0:tokens, :] = y.astype(BF16)
        for s, first in enumerate((0, rows - HALO)):
            parts = []
            for f in range(frames):
                a = (f * rows + first) * columns
                parts.append(y[a : a + HALO * columns])
            rsend[s, i] = jnp.concatenate(parts, axis=0).astype(BF16)

    def clear(where, first, count):
        @pl.when(jnp.logical_not(where))
        def _():
            kvext[:, first : first + count, :] = jnp.zeros((2, count, width), BF16)

    clear(before_t, early, wing)
    clear(after_t, later, wing)
    clear(before_h, up, strip)
    clear(after_h, down, strip)
    for base in (early, later):
        clear(before_h, base + side_rows, corner)
        clear(after_h, base + side_rows + corner, corner)

    piece = table_ref[0:1, :]
    hit = jnp.ones_like(piece)
    for s, (df, dr) in enumerate(ORDER):
        a, b = t + df, h + dr
        inside = (a >= 0) & (a < nt) & (b >= 0) & (b < nh)
        here = jnp.where(inside, valid_ref[lax.rem(a + nt, nt), lax.rem(b + nh, nh)], 0)
        hit = jnp.where(piece == s + 1, here, hit)
    near = (table_ref[1:2, :] <= reach_ref[t, 0, h]) & (table_ref[2:3, :] <= reach_ref[t, 1, h])
    bias[...] = jnp.where((piece == 0) | (near & (hit == 1)), 0.0, -1e30)

    loads[2].wait()
    ogown[...] = og4[...].reshape(tokens, model)
    loads[3].wait()

    row_copies = (
        (before_h, after_h, remote(
            rsend.at[0], kvext.at[:, pl.ds(down, strip), :], row_s.at[0], row_r.at[0],
            (t, lax.rem(h + nh - 1, nh)))),
        (after_h, before_h, remote(
            rsend.at[1], kvext.at[:, pl.ds(up, strip), :], row_s.at[1], row_r.at[1],
            (t, lax.rem(h + 1, nh)))),
    )
    prev_t, next_t = (lax.rem(t + nt - 1, nt), h), (lax.rem(t + 1, nt), h)
    frame_copies = (
        (before_t, after_t, remote(
            kvext.at[:, pl.ds(0, side_rows), :], kvext.at[:, pl.ds(later, side_rows), :],
            fr_s.at[0], fr_r.at[0], prev_t)),
        (after_t, before_t, remote(
            kvext.at[:, pl.ds(tokens - side_rows, side_rows), :],
            kvext.at[:, pl.ds(early, side_rows), :], fr_s.at[1], fr_r.at[1], next_t)),
    )
    corner_copies = []
    for i, (base, here) in enumerate(((up, before_h), (down, after_h))):
        shift = side_rows + i * corner
        corner_copies.append((before_t & here, after_t & here, remote(
            kvext.at[:, pl.ds(base, corner), :], kvext.at[:, pl.ds(later + shift, corner), :],
            co_s.at[2 * i], co_r.at[2 * i], prev_t)))
        corner_copies.append((after_t & here, before_t & here, remote(
            kvext.at[:, pl.ds(base + strip - corner, corner), :],
            kvext.at[:, pl.ds(early + shift, corner), :],
            co_s.at[2 * i + 1], co_r.at[2 * i + 1], next_t)))

    def begin(copies):
        for send, _, copy in copies:
            pl.when(send)(copy.start)

    def finish(copies):
        for send, recv, copy in copies:
            pl.when(send)(copy.wait_send)
            pl.when(recv)(copy.wait_recv)

    def w_block(p, part):
        return wfull.at[pl.ds(pl.multiple_of(at(p) * share + part * cut, 16), cut), mine]

    def w_copy(i, side):
        part = i % 2 if side == 0 else 1 - i % 2
        ref = w_block(pos + (2 * side - 1) * (i // 2), part)
        return remote(ref, ref, w_s.at[side, i], w_r.at[side, i], (right, left)[side])

    def w_share(i, side):
        part = i % 2 if side == 0 else 1 - i % 2
        ref = w_block(pos + (2 * side - 1) * (i // 2 + 1), part)
        return remote(ref, ref, sh_s.at[side, i], sh_r.at[side, i], partner)

    def w_poll(i):
        for side in range(2):
            w_copy(i, side).wait()
            if i + 2 < slots:
                w_copy(i + 2, side).start()
            w_share(i, side).start()

    pl.semaphore_wait(barrier, len(peers))
    begin(row_copies)
    begin(frame_copies)
    for i in range(2):
        for side in range(2):
            w_copy(i, side).start()
    og_across = remote(
        ogown.at[:, ycols], og2.at[pl.ds(tokens, tokens), :], og_s.at[0], og_r.at[0], across
    )
    og_across.start()
    loads[4].wait()
    q2[...] = in4[2].reshape(tokens, width)
    og2[0:tokens, :] = ogown[:, xcols]
    finish(row_copies)
    begin(corner_copies)
    w_poll(0)
    finish(frame_copies)
    finish(corner_copies)

    def nt_dot(a, b):
        return lax.dot_general(a, b, (((1,), (1,)), ((), ())), preferred_element_type=F32)

    def tn_dot(a, b):
        return lax.dot_general(a, b, (((0,), (0,)), ((), ())), preferred_element_type=F32)

    def nn_dot(a, b):
        return lax.dot_general(a, b, (((1,), (0,)), ((), ())), preferred_element_type=F32)

    def head(g, j):
        return pl.ds(pl.multiple_of(g * gsize + j * HEAD_DIM, HEAD_DIM), HEAD_DIM)

    def mix_copy(g, kind):
        if kind == 0:
            return remote(
                mix.at[pl.ds(0, tokens), gcols(g)], mix.at[pl.ds(tokens, tokens), gcols(g)],
                mx_s.at[g], mx_r.at[g], across)
        first = (kind - 1) * tokens
        return remote(
            mix.at[pl.ds(first, tokens), gcols(g)],
            mix.at[pl.ds(2 * tokens + first, tokens), gcols(g)],
            mc_s.at[kind - 1, g], mc_r.at[kind - 1, g], partner)

    def forward(g):
        for j in range(gheads):
            cs = head(g, j)
            scores = nt_dot(q2[:, cs], kvext[0, :, cs]) * scale + bias[...]
            e = jnp.exp(scores - jnp.max(scores, axis=-1, keepdims=True))
            p = e * (1.0 / jnp.sum(e, axis=-1, keepdims=True))
            prob[g * gheads + j] = p
            mix[0:tokens, cs] = nn_dot(p.astype(BF16), kvext[1, :, cs]).astype(BF16)
        mix_copy(g, 0).start()
        mix_copy(g, 1).start()

    for g in range(groups):
        forward(g)
        if g == 1:
            og_across.wait()
            ogc[0 : 2 * tokens, :] = og2[:, mine]
            og_core = remote(
                og2.at[:, other], ogc.at[pl.ds(2 * tokens, 2 * tokens), :],
                og_s.at[1], og_r.at[1], partner)
            og_core.start()
        if g > 0:
            mix_copy(g - 1, 0).wait()
            mix_copy(g - 1, 2).start()
        w_poll(g + 1)
    mix_copy(groups - 1, 0).wait()
    mix_copy(groups - 1, 2).start()
    og_core.wait()
    for g in range(groups):
        mix_copy(g, 1).wait()
        mix_copy(g, 2).wait()

    def weight(g):
        span = pl.ds(pl.multiple_of(g * gsize, 128), gsize)
        gpart[span, :] = tn_dot(mix[:, span], ogc[...])

    def gw_copy(j, side):
        return remote(
            gws.at[side, j], gwr.at[side, j], gw_s.at[side, j], gw_r.at[side, j],
            (right, left)[side])

    def gw_send(j, side):
        part = j % 2 if side == 0 else 1 - j % 2
        blk = at(pos + (1 - 2 * side) * (nh // 2 - (j + 1) // 2))
        total = gpart[pl.ds(pl.multiple_of(blk * share + part * cut, 16), cut), :]
        if j >= 2:
            total += gwr[side, j - 2].astype(F32)
        gws[side, j] = total.astype(BF16)
        gw_copy(j, side).start()

    def gw_poll(j):
        for side in range(2):
            gw_copy(j, side).wait()
            if j + 2 < slots:
                gw_send(j + 2, side)

    zfar = groups - 1 - h // 2
    weight(zfar)
    for side in range(2):
        gw_send(0, side)
    w_poll(5)

    def rest(i, carry):
        weight(lax.rem(zfar + 1 + i, groups))
        return carry

    lax.fori_loop(0, groups - 1, rest, 0)
    for side in range(2):
        gw_send(1, side)
    w_poll(6)
    for i in range(slots):
        for side in range(2):
            w_share(i, side).wait()

    def dm_copy(g):
        return remote(
            dms.at[:, gcols(g)], dmr.at[:, gcols(g)], dm_s.at[g], dm_r.at[g], across)

    def project(g, carry):
        both = nt_dot(og2[...], wfull[gcols(g), :])
        dmx[:, gcols(g)] = both[:tokens]
        dms[:, gcols(g)] = both[tokens:].astype(BF16)
        dm_copy(g).start()
        return carry

    lax.fori_loop(0, groups, project, 0)

    def attn(i, carry):
        cs = pl.ds(pl.multiple_of(i * 256, 256), 256)
        both = nn_dot(mix[0 : 2 * tokens, :], wfull[:, cs])
        attn2[:, pl.ds(pl.multiple_of(x * half + i * 256, 256), 256)] = both[:tokens].astype(BF16)
        asend[:, cs] = both[tokens:].astype(BF16)
        return carry

    lax.fori_loop(0, half // 256, attn, 0)
    gw_poll(0)

    def wing_copies(g):
        return (
            (before_t, after_t, remote(
                gsend.at[:, pl.ds(0, wing), gcols(g)], grecv.at[0, :, :, gcols(g)],
                g1_s.at[0, g], g1_r.at[0, g], prev_t)),
            (after_t, before_t, remote(
                gsend.at[:, pl.ds(wing, wing), gcols(g)], grecv.at[1, :, :, gcols(g)],
                g1_s.at[1, g], g1_r.at[1, g], next_t)),
        )

    def backward(g):
        dm_copy(g).wait()
        for j in range(gheads):
            cs = head(g, j)
            p = prob[g * gheads + j]
            dm = (dmx[:, cs] + dmr[:, cs].astype(F32)).astype(BF16)
            dp = nt_dot(dm, kvext[1, :, cs])
            inner = jnp.sum(p * dp, axis=-1, keepdims=True)
            ds = (p * (dp - inner) * scale).astype(BF16)
            dq2[:, cs] = nn_dot(ds, kvext[0, :, cs]).astype(BF16)
            for i, grad in enumerate((tn_dot(ds, q2[:, cs]), tn_dot(p.astype(BF16), dm))):
                acc[i, :, cs] = grad[:tokens]
                gsend[i, 0:nwing, cs] = grad[tokens : tokens + nwing].astype(BF16)
                ud[i, :, cs] = grad[tokens + nwing :]
        begin(wing_copies(g))

    for g in range(groups):
        backward(g)
        if g > 0:
            gw_poll(g)
    attn_across = remote(asend, attn2.at[:, xcols], at_s.at[0], at_r.at[0], across)
    attn_across.start()
    dq_ref[...] = dq2[...].reshape(*tile, width)

    def strip_copies(g):
        return (
            (before_h, after_h, remote(
                gsend.at[:, pl.ds(nwing, strip), gcols(g)], rrecv.at[0, :, :, gcols(g)],
                g2_s.at[0, g], g2_r.at[0, g], (t, lax.rem(h + nh - 1, nh)))),
            (after_h, before_h, remote(
                gsend.at[:, pl.ds(nwing + strip, strip), gcols(g)], rrecv.at[1, :, :, gcols(g)],
                g2_s.at[1, g], g2_r.at[1, g], (t, lax.rem(h + 1, nh)))),
        )

    def fold(g, carry):
        cs = gcols(g)
        finish(wing_copies(g))
        for s, (here, tok, edge) in enumerate(
            ((after_t, tokens - side_rows, strip - corner), (before_t, 0, 0))
        ):
            @pl.when(here)
            def _():
                for i in range(2):
                    y = grecv[s, i, :, cs].astype(F32)
                    acc[i, tok : tok + side_rows, cs] += y[:side_rows]
                    ud[i, edge : edge + corner, cs] += y[side_rows : side_rows + corner]
                    ud[i, strip + edge : strip + edge + corner, cs] += y[side_rows + corner :]

        for i in range(2):
            gsend[i, nwing:, cs] = ud[i, :, cs].astype(BF16)
        begin(strip_copies(g))
        return carry

    lax.fori_loop(0, groups, fold, 0)
    gw_poll(4)
    for g in range(groups):
        finish(strip_copies(g))
    for i, ref in enumerate((dk_ref, dv_ref)):
        for s, (here, first) in enumerate(((after_h, rows - HALO), (before_h, 0))):
            @pl.when(here)
            def _():
                y = rrecv[s, i].astype(F32)
                for f in range(frames):
                    a = (f * rows + first) * columns
                    n = HALO * columns
                    acc[i, a : a + n, :] += y[f * n : (f + 1) * n]

        ref[...] = acc[i].astype(BF16).reshape(*tile, width)
    gw_poll(5)
    attn_across.wait()
    attn_ref[...] = attn2[...].reshape(*tile, model)
    gw_poll(6)
    for part in range(2):
        base = pl.multiple_of(h * share + part * cut, 16)
        gw_ref[part * cut : (part + 1) * cut, :] = (
            gpart[pl.ds(base, cut), :]
            + gwr[0, slots - 1 - part].astype(F32)
            + gwr[1, slots - 2 + part].astype(F32)
        )


def paired(nt, nh, queries, key_tokens, value_tokens, out_weight, out_grad, window_reach, tile_valid):
    frames, rows, columns, width = queries.shape
    model = out_grad.shape[3]
    share = out_weight.shape[0]
    tokens = frames * rows * columns
    heads = width // HEAD_DIM
    halo = sum(piece_sizes(frames, rows, columns))
    strip = frames * HALO * columns
    wing = HALO * rows * columns + 2 * HALO * HALO * columns
    ext = tokens + halo
    table = key_table(frames, rows, columns, ORDER)
    half, quarter, cut, slots = model // 2, model // 4, share // 2, nh - 1
    vmem = pl.BlockSpec(memory_space=pltpu.VMEM)
    smem = pl.BlockSpec(memory_space=pltpu.SMEM)
    hbm = pl.BlockSpec(memory_space=pl.ANY)
    dma = pltpu.SemaphoreType.DMA
    tile = (frames, rows, columns)
    return pl.pallas_call(
        functools.partial(paired_kernel, (nt, nh, frames, rows, columns)),
        out_shape=(
            jax.ShapeDtypeStruct((*tile, model), BF16),
            jax.ShapeDtypeStruct((*tile, width), BF16),
            jax.ShapeDtypeStruct((*tile, width), BF16),
            jax.ShapeDtypeStruct((*tile, width), BF16),
            jax.ShapeDtypeStruct((share, quarter), F32),
        ),
        in_specs=[hbm, hbm, hbm, hbm, hbm, vmem, smem, smem],
        out_specs=[vmem] * 5,
        scratch_shapes=[
            pltpu.VMEM((3, *tile, width), BF16),
            pltpu.VMEM((*tile, model), BF16),
            pltpu.VMEM((tokens, width), BF16),
            pltpu.VMEM((tokens, width), BF16),
            pltpu.VMEM((2, ext, width), BF16),
            pltpu.VMEM((2, 2, strip, width), BF16),
            pltpu.VMEM((width, half), BF16),
            pltpu.VMEM((tokens, model), BF16),
            pltpu.VMEM((2 * tokens, half), BF16),
            pltpu.VMEM((4 * tokens, quarter), BF16),
            pltpu.VMEM((heads, tokens, ext), F32),
            pltpu.VMEM((4 * tokens, width), BF16),
            pltpu.VMEM((tokens, width), F32),
            pltpu.VMEM((tokens, width), BF16),
            pltpu.VMEM((tokens, width), BF16),
            pltpu.VMEM((tokens, model), BF16),
            pltpu.VMEM((tokens, half), BF16),
            pltpu.VMEM((2, tokens, width), F32),
            pltpu.VMEM((2, 2 * strip, width), F32),
            pltpu.VMEM((2, halo, width), BF16),
            pltpu.VMEM((2, 2, wing, width), BF16),
            pltpu.VMEM((2, 2, strip, width), BF16),
            pltpu.VMEM((width, quarter), F32),
            pltpu.VMEM((2, slots, cut, quarter), BF16),
            pltpu.VMEM((2, slots, cut, quarter), BF16),
            pltpu.VMEM((1, ext), F32),
            dma((5,)), dma((2,)), dma((2,)), dma((2,)), dma((2,)), dma((4,)), dma((4,)),
            dma((2, slots)), dma((2, slots)), dma((2, slots)), dma((2, slots)),
            dma((2,)), dma((2,)), dma((4,)), dma((4,)), dma((2, 4)), dma((2, 4)),
            dma((4,)), dma((4,)), dma((1,)), dma((1,)),
            dma((2, 4)), dma((2, 4)), dma((2, 4)), dma((2, 4)), dma((2, slots)), dma((2, slots)),
        ],
        compiler_params=pltpu.CompilerParams(
            collective_id=1, has_side_effects=True, vmem_limit_bytes=56 * 2**20
        ),
    )(
        queries, key_tokens, value_tokens, out_grad, out_weight, table,
        jnp.transpose(window_reach, (0, 2, 1)), tile_valid,
    )


def solution(mesh):
    tile = P("tm", "height", None, None)
    nt, nh = mesh.shape["tm"], mesh.shape["height"]
    body = paired if (nt, nh) == (4, 8) else shards
    return jax.shard_map(
        functools.partial(body, nt, nh),
        mesh=mesh,
        in_specs=(tile, tile, tile, P("height", None), tile, P(), P()),
        out_specs=(tile, tile, tile, tile, P("height", "tm")),
        check_vma=False,
    )
```

```python
import functools
import math

import jax
import jax.numpy as jnp
import numpy as np
from jax import lax
from jax.experimental import pallas as pl
from jax.experimental.pallas import tpu as pltpu
from jax.sharding import PartitionSpec as P

HEAD_DIM = 128
HALO = 2
MESH = pl.DeviceIdType.MESH
F32 = jnp.float32
BF16 = jnp.bfloat16
SIDES = ((-1, 0), (1, 0), (0, -1), (0, 1), (-1, -1), (-1, 1), (1, -1), (1, 1))


def piece_sizes(frames, rows, columns):
    sizes = []
    for df, dr in SIDES:
        sizes.append((HALO if df else frames) * (HALO if dr else rows) * columns)
    return sizes


def key_table(frames, rows, columns, sides=SIDES):
    table = []
    for piece, (df, dr) in enumerate(((0, 0),) + sides):
        for f in range(HALO) if df else range(frames):
            for r in range(HALO) if dr else range(rows):
                fd = 0 if df == 0 else (HALO - f if df < 0 else f + 1)
                rd = 0 if dr == 0 else (HALO - r if dr < 0 else r + 1)
                table += [(piece, fd, rd)] * columns
    return np.ascontiguousarray(np.array(table, np.int32).T)


def piece_rows(df, dr, frames, rows, columns):
    fs = range(frames) if df == 0 else (range(frames - HALO, frames) if df < 0 else range(HALO))
    if dr == 0:
        return [(fs[0] * rows * columns, len(fs) * rows * columns)]
    first = (rows - HALO) if dr < 0 else 0
    return [((f * rows + first) * columns, HALO * columns) for f in fs]


def kernel(
    dims,
    q_ref, k_ref, v_ref, table_ref, reach_ref, valid_ref, w_hbm, og_hbm,
    attn_ref, dq_ref, dk_ref, dv_ref, gw_ref,
    wfull, ogown, ogcols, kvsend, kvext, gsend, grecv, prob, dmixed, mixed, mixall, acc, gpart, bias_ref, gwsend, gwrecv,
    local_sem, halo_s, halo_r, grad_s, grad_r, mix_s, mix_r,
    wr_s, wr_r, wl_s, wl_r, wc_s, wc_r, og_s, og_r, gw_s, gw_r,
):
    nt, nh, frames, rows, columns = dims
    t, h = lax.axis_index("tm"), lax.axis_index("height")
    tokens, width = q_ref.shape
    model = og_hbm.shape[1]
    share = w_hbm.shape[0]
    heads = width // HEAD_DIM
    half = model // 2
    window = gpart.shape[1]
    span_cols = model // nt
    scale = 1.0 / math.sqrt(HEAD_DIM)
    sizes = piece_sizes(frames, rows, columns)
    starts = [sum(sizes[:i]) for i in range(8)]

    def place(df, dr):
        return (lax.rem(t + nt + df, nt), lax.rem(h + nh + dr, nh))

    def exists(df, dr):
        a, b = t + df, h + dr
        return (a >= 0) & (a < nt) & (b >= 0) & (b < nh)

    def exchange(copies, sign, action):
        for (df, dr), copy in zip(SIDES, copies):
            if action == "start":
                pl.when(exists(sign * df, sign * dr))(copy.start)
            else:
                pl.when(exists(sign * df, sign * dr))(copy.wait_send)
                pl.when(exists(-sign * df, -sign * dr))(copy.wait_recv)

    def remote(src, dst, ssem, rsem, where):
        return pltpu.make_async_remote_copy(
            src_ref=src, dst_ref=dst, send_sem=ssem, recv_sem=rsem,
            device_id=where, device_id_type=MESH,
        )

    def wrow(j, lo=0, size=None):
        return pl.ds(pl.multiple_of(j * share + lo, 16), share if size is None else size)

    def orow(j, lo=0, size=None):
        return pl.ds(pl.multiple_of(j * tokens + lo, 16), tokens if size is None else size)

    own_w = pltpu.make_async_copy(w_hbm, wfull.at[wrow(h), :], local_sem.at[0])
    own_og = pltpu.make_async_copy(og_hbm, ogown, local_sem.at[1])
    own_w.start()
    own_og.start()

    barrier = pltpu.get_barrier_semaphore()
    greeted = 0
    for i in range(1, nh):
        pl.semaphore_signal(barrier, inc=1, device_id=(t, lax.rem(h + i, nh)), device_id_type=MESH)
        greeted += 1
    for i in range(1, nt):
        pl.semaphore_signal(barrier, inc=1, device_id=(lax.rem(t + i, nt), h), device_id_type=MESH)
        greeted += 1
    for df, dr in SIDES:
        if df and dr:
            pl.semaphore_signal(barrier, inc=1, device_id=place(df, dr), device_id_type=MESH)
            greeted += 1

    piece = table_ref[0:1, :]
    hit = jnp.ones_like(piece)
    for s, (df, dr) in enumerate(SIDES):
        a, b = place(df, dr)
        here = jnp.where(exists(df, dr), valid_ref[a, b], 0)
        hit = jnp.where(piece == s + 1, here, hit)
    near = (table_ref[1:2, :] <= reach_ref[t, h, 0]) & (table_ref[2:3, :] <= reach_ref[t, h, 1])
    bias_ref[...] = jnp.where((piece == 0) | (near & (hit == 1)), 0.0, -1e30)

    for i, ref in enumerate((k_ref, v_ref)):
        x = ref[...]
        kvext[i, 0:tokens, :] = x
        x = x.astype(F32)
        for s, (df, dr) in enumerate(SIDES):
            parts = [x[a : a + n] for a, n in piece_rows(df, dr, frames, rows, columns)]
            y = parts[0] if len(parts) == 1 else jnp.concatenate(parts, axis=0)
            kvsend[i, starts[s] : starts[s] + sizes[s], :] = y.astype(BF16)

    for s, (df, dr) in enumerate(SIDES):

        @pl.when(jnp.logical_not(exists(df, dr)))
        def _():
            rs = pl.ds(tokens + starts[s], sizes[s])
            kvext[:, rs, :] = jnp.zeros((2, sizes[s], width), BF16)

    par = lax.rem(h, 2)
    pos = (1 - par) * (h // 2) + par * (nh - 1 - h // 2)

    def at(p):
        p = lax.rem(p + nh, nh)
        far = p // (nh // 2)
        return (1 - far) * (2 * p) + far * (2 * (nh - 1 - p) + 1)

    right, left = (t, at(pos + 1)), (t, at(pos - 1))
    steps = nh // 2
    core = lax.rem(t, 2)
    partner = (t + 1 - 2 * core, h)
    mine = pl.ds(pl.multiple_of(core * half, 128), half)

    def span(step, size, side):
        if step < steps - 1:
            return 0, size
        return (0 if side == 0 else size // 2), size // 2

    def ring_sends(step, buf, rowfn, size, cols, sems):
        out = []
        for side, (target, sign) in enumerate(((right, -1), (left, 1))):
            lo, n = span(step, size, side)
            ref = buf.at[rowfn(at(pos + sign * step), lo, n), cols]
            ssem, rsem = sems[2 * side], sems[2 * side + 1]
            copy = remote(ref, ref, ssem.at[step], rsem.at[step], target)
            copy.start()
            out.append(copy)
        return out

    wsems = (wr_s, wr_r, wl_s, wl_r)
    def w_sends(step):
        return ring_sends(step, wfull, wrow, share, mine, wsems)

    def gw_sends(step):
        out = []
        for side, (target, sign) in enumerate(((right, 1), (left, -1))):
            base = at(pos + sign * (steps - step)) * share
            cut = share // 2
            for part in range(2):
                if step == 0 and part != side:
                    continue
                rs = slice(part * cut, (part + 1) * cut)
                total = gpart[pl.ds(pl.multiple_of(base + part * cut, 16), cut), :]
                if step > 1 or (step == 1 and part == side):
                    total += gwrecv[side, step - 1, rs, :].astype(F32)
                gwsend[side, step, rs, :] = total.astype(BF16)
            rs = pl.ds(side * cut, cut) if step == 0 else pl.ds(0, share)
            i = side * steps + step
            copy = remote(
                gwsend.at[side, step, rs, :], gwrecv.at[side, step, rs, :],
                gw_s.at[i], gw_r.at[i], target,
            )
            copy.start()
            out.append(copy)
        return out

    def cols_start(j):
        block = jnp.minimum((j * span_cols) // 128, (model - window) // 128)
        return pl.multiple_of(block * 128, 128)

    def share_sends(step):
        out = []
        for side, sign in enumerate((-1, 1)):
            lo, n = span(step, share, side)
            ref = wfull.at[wrow(at(pos + sign * (step + 1)), lo, n), mine]
            i = 2 * step + side
            out.append(remote(ref, ref, wc_s.at[i], wc_r.at[i], partner))
        for copy in out:
            copy.start()
        return out

    own_w.wait()
    own_og.wait()
    pl.semaphore_wait(barrier, greeted)
    halos = []
    for s, (df, dr) in enumerate(SIDES):
        copy = remote(
            kvsend.at[:, pl.ds(starts[s], sizes[s]), :],
            kvext.at[:, pl.ds(tokens + starts[s], sizes[s]), :],
            halo_s.at[s], halo_r.at[s], place(-df, -dr),
        )
        halos.append(copy)
    exchange(halos, -1, "start")
    live = w_sends(0)
    ogcols[orow(t), :] = ogown[:, pl.ds(cols_start(t), window)]
    gathers = []
    for i in range(1, nt):
        j = lax.rem(t + i, nt)
        copy = remote(
            ogown.at[:, pl.ds(cols_start(j), window)], ogcols.at[orow(t), :],
            og_s.at[i - 1], og_r.at[i - 1], (j, h),
        )
        copy.start()
        gathers.append(copy)
    shared = []

    def w_step(step):
        for copy in live:
            copy.wait()
        live.clear()
        if step < steps - 1:
            live.extend(w_sends(step + 1))
        shared.extend(share_sends(step))

    for step in range(2):
        w_step(step)
    exchange(halos, -1, "wait")

    group = 3 if heads % 3 == 0 else 1

    def cols_of(c):
        return pl.ds(pl.multiple_of(c * HEAD_DIM, HEAD_DIM), HEAD_DIM)

    def nt_dot(a, b):
        return lax.dot_general(a, b, (((1,), (1,)), ((), ())), preferred_element_type=F32)

    def tn_dot(a, b):
        return lax.dot_general(a, b, (((0,), (0,)), ((), ())), preferred_element_type=F32)

    def nn_dot(a, b):
        return lax.dot_general(a, b, (((1,), (0,)), ((), ())), preferred_element_type=F32)

    def forward(g, carry):
        for j in range(group):
            c = g * group + j
            cs = cols_of(c)
            scores = nt_dot(q_ref[:, cs], kvext[0, :, cs]) * scale + bias_ref[...]
            e = jnp.exp(scores - jnp.max(scores, axis=-1, keepdims=True))
            p = e / jnp.sum(e, axis=-1, keepdims=True)
            prob[c] = p
            mixed[:, cs] = nn_dot(p.astype(BF16), kvext[1, :, cs]).astype(BF16)
        return carry

    lax.fori_loop(0, heads // group, forward, 0)

    mixall[orow(t), :] = mixed[...]
    for i in range(1, nt):
        copy = remote(
            mixed, mixall.at[orow(t), :], mix_s.at[i - 1], mix_r.at[i - 1],
            (lax.rem(t + i, nt), h),
        )
        copy.start()
        gathers.append(copy)

    def gw_step(step):
        for copy in live:
            copy.wait()
        live.clear()
        if step < steps:
            live.extend(gw_sends(step))

    for step in range(2, steps):
        w_step(step)

    for copy in gathers:
        copy.wait()

    def weight(i, carry):
        cs = pl.ds(pl.multiple_of(i * 256, 256), 256)
        gpart[cs, :] = tn_dot(mixall[:, cs], ogcols[...])
        return carry

    lax.fori_loop(0, width // 256, weight, 0)
    gw_step(0)
    for copy in shared:
        copy.wait()

    def project(i, carry):
        r = pl.ds(pl.multiple_of(i * 256, 256), 256)
        dmixed[:, r] = nt_dot(ogown[...], wfull[r, :]).astype(BF16)
        return carry

    lax.fori_loop(0, width // 256, project, 0)

    gw_step(1)

    def backward(g, carry):
        for j in range(group):
            c = g * group + j
            cs = cols_of(c)
            p = prob[c]
            dm = dmixed[:, cs]
            dp = nt_dot(dm, kvext[1, :, cs])
            inner = jnp.sum(p * dp, axis=-1, keepdims=True)
            ds = (p * (dp - inner) * scale).astype(BF16)
            dq_ref[:, cs] = nn_dot(ds, kvext[0, :, cs]).astype(BF16)
            dk = tn_dot(ds, q_ref[:, cs])
            dv = tn_dot(p.astype(BF16), dm)
            acc[0, :, cs] = dk[:tokens]
            acc[1, :, cs] = dv[:tokens]
            gsend[0, :, cs] = dk[tokens:].astype(BF16)
            gsend[1, :, cs] = dv[tokens:].astype(BF16)
        return carry

    lax.fori_loop(0, heads // group, backward, 0)

    grads = []
    for s, (df, dr) in enumerate(SIDES):
        rs = pl.ds(starts[s], sizes[s])
        copy = remote(
            gsend.at[:, rs, :], grecv.at[:, rs, :], grad_s.at[s], grad_r.at[s], place(df, dr)
        )
        grads.append(copy)
    exchange(grads, 1, "start")
    gw_step(2)

    def attn(i, carry):
        cs = pl.ds(pl.multiple_of(i * 256, 256), 256)
        attn_ref[:, cs] = nn_dot(mixed[...], wfull[:, cs]).astype(BF16)
        return carry

    lax.fori_loop(0, model // 256, attn, 0)
    gw_step(3)

    exchange(grads, 1, "wait")
    for i, ref in enumerate((dk_ref, dv_ref)):
        for s, (df, dr) in enumerate(SIDES):

            @pl.when(exists(-df, -dr))
            def _():
                y = grecv[i, starts[s] : starts[s] + sizes[s], :].astype(F32)
                first = 0
                for a, n in piece_rows(df, dr, frames, rows, columns):
                    acc[i, a : a + n, :] += y[first : first + n]
                    first += n

        ref[...] = acc[i].astype(BF16)

    for step in range(4, steps + 1):
        gw_step(step)
    gw_ref[...] = (
        gpart[wrow(h), :]
        + gwrecv[0, steps - 1].astype(F32)
        + gwrecv[1, steps - 1].astype(F32)
    )


def shards(nt, nh, queries, key_tokens, value_tokens, out_weight, out_grad, window_reach, tile_valid):
    frames, rows, columns, width = queries.shape
    model = out_grad.shape[3]
    share = out_weight.shape[0]
    tokens = frames * rows * columns
    heads = width // HEAD_DIM
    halo = sum(piece_sizes(frames, rows, columns))
    ext = tokens + halo
    table = key_table(frames, rows, columns)
    narrow = (model // nt) % 128 == 0
    block = model // nt if narrow else 256
    steps = nh // 2
    vmem = pl.BlockSpec(memory_space=pltpu.VMEM)
    smem = pl.BlockSpec(memory_space=pltpu.SMEM)
    hbm = pl.BlockSpec(memory_space=pl.ANY)
    dma = pltpu.SemaphoreType.DMA
    attn, dq, dk, dv, gw = pl.pallas_call(
        functools.partial(kernel, (nt, nh, frames, rows, columns)),
        out_shape=(
            jax.ShapeDtypeStruct((tokens, model), BF16),
            jax.ShapeDtypeStruct((tokens, width), BF16),
            jax.ShapeDtypeStruct((tokens, width), BF16),
            jax.ShapeDtypeStruct((tokens, width), BF16),
            jax.ShapeDtypeStruct((share, block), F32),
        ),
        in_specs=[vmem, vmem, vmem, vmem, smem, smem, hbm, hbm],
        out_specs=[vmem] * 5,
        scratch_shapes=[
            pltpu.VMEM((width, model), BF16),
            pltpu.VMEM((tokens, model), BF16),
            pltpu.VMEM((nt * tokens, block), BF16),
            pltpu.VMEM((2, halo, width), BF16),
            pltpu.VMEM((2, ext, width), BF16),
            pltpu.VMEM((2, halo, width), BF16),
            pltpu.VMEM((2, halo, width), BF16),
            pltpu.VMEM((heads, tokens, ext), F32),
            pltpu.VMEM((tokens, width), BF16),
            pltpu.VMEM((tokens, width), BF16),
            pltpu.VMEM((nt * tokens, width), BF16),
            pltpu.VMEM((2, tokens, width), F32),
            pltpu.VMEM((width, block), F32),
            pltpu.VMEM((1, ext), F32),
            pltpu.VMEM((2, steps, share, block), BF16),
            pltpu.VMEM((2, steps, share, block), BF16),
            dma((2,)), dma((8,)), dma((8,)), dma((8,)), dma((8,)),
            dma((nt - 1,)), dma((nt - 1,)),
            dma((steps,)), dma((steps,)), dma((steps,)), dma((steps,)),
            dma((2 * steps,)), dma((2 * steps,)),
            dma((nt - 1,)), dma((nt - 1,)), dma((2 * steps,)), dma((2 * steps,)),
        ],
        compiler_params=pltpu.CompilerParams(
            collective_id=0, has_side_effects=True, vmem_limit_bytes=56 * 2**20
        ),
    )(
        queries.reshape(tokens, width),
        key_tokens.reshape(tokens, width),
        value_tokens.reshape(tokens, width),
        table,
        window_reach,
        tile_valid,
        out_weight,
        out_grad.reshape(tokens, model),
    )
    if not narrow:
        size = model // nt
        at = lax.axis_index("tm") * size
        first = jnp.minimum(at // 128, (model - block) // 128) * 128
        gw = lax.dynamic_slice_in_dim(gw, at - first, size, axis=1)
    tile = (frames, rows, columns)
    return (
        attn.reshape(*tile, model),
        dq.reshape(*tile, width),
        dk.reshape(*tile, width),
        dv.reshape(*tile, width),
        gw,
    )


ORDER = ((-1, 0), (-1, -1), (-1, 1), (1, 0), (1, -1), (1, 1), (0, -1), (0, 1))


def paired_kernel(
    dims,
    q_hbm, k_hbm, v_hbm, og_hbm, w_hbm, table_ref, reach_ref, valid_ref,
    attn_hbm, dq_hbm, dk_hbm, dv_hbm, gw_hbm,
    attn_ref, dq_ref, dk_ref, dv_ref, gw_ref, in4, og4, q2, dq2, kvext, rsend, wfull, ogown, og2, ogc, prob, mix, dmx, dms, dmr, attn2, asend,
    acc, ud, gsend, grecv, rrecv, kvpass, gpass, gpart, gws, gwr, bias,
    ld, out, kp_s, kp_r, gp_s, gp_r, row_s, row_r, fr_s, fr_r, co_s, co_r, w_s, w_r, sh_s, sh_r, og_s, og_r, mx_s, mx_r,
    mc_s, mc_r, dm_s, dm_r, at_s, at_r, g1_s, g1_r, g2_s, g2_r, gw_s, gw_r,
):
    nt, nh, frames, rows, columns = dims
    t, h = lax.axis_index("tm"), lax.axis_index("height")
    tokens, width = q2.shape
    model = ogown.shape[1]
    share = w_hbm.shape[0]
    half, quarter = model // 2, model // 4
    cut = share // 2
    groups = 4
    gsize = width // groups
    gheads = gsize // HEAD_DIM
    tile = (frames, rows, columns)
    scale = 1.0 / math.sqrt(HEAD_DIM)
    x, core = t // 2, lax.rem(t, 2)
    partner = (t + 1 - 2 * core, h)
    across = (lax.rem(t + 2, nt), h)
    side_rows = HALO * rows * columns
    corner = HALO * HALO * columns
    strip = frames * HALO * columns
    wing = side_rows + 2 * corner
    nwing = 2 * wing
    early, later = tokens, tokens + wing
    up, down = tokens + 2 * wing, tokens + 2 * wing + strip
    before_t, after_t, before_h, after_h = t > 0, t < nt - 1, h > 0, h < nh - 1
    down_src, down_mid = h == 2, h == 3
    up_src, up_mid = h == nh - 3, h == nh - 4
    prev_t, next_t = (lax.rem(t + nt - 1, nt), h), (lax.rem(t + 1, nt), h)
    prev_h, next_h = (t, lax.rem(h + nh - 1, nh)), (t, lax.rem(h + 1, nh))
    prev2_h, next2_h = (t, lax.rem(h + nh - 2, nh)), (t, lax.rem(h + 2, nh))

    def remote(src, dst, ssem, rsem, where):
        return pltpu.make_async_remote_copy(
            src_ref=src, dst_ref=dst, send_sem=ssem, recv_sem=rsem,
            device_id=where, device_id_type=MESH,
        )

    def gcols(g):
        return pl.ds(pl.multiple_of(g * gsize, 128), gsize)

    par = lax.rem(h, 2)
    pos = (1 - par) * (h // 2) + par * (nh - 1 - h // 2)

    def at(p):
        p = lax.rem(p + nh, nh)
        far = p // (nh // 2)
        return (1 - far) * (2 * p) + far * (2 * (nh - 1 - p) + 1)

    right, left = (t, at(pos + 1)), (t, at(pos - 1))
    mine = pl.ds(pl.multiple_of(core * quarter, 128), quarter)
    other = pl.ds(pl.multiple_of((1 - core) * quarter, 128), quarter)
    xcols = pl.ds(pl.multiple_of(x * half, 128), half)
    ycols = pl.ds(pl.multiple_of((1 - x) * half, 128), half)
    slots = nh - 1

    loads = [
        pltpu.make_async_copy(k_hbm, in4.at[0], ld.at[0]),
        pltpu.make_async_copy(v_hbm, in4.at[1], ld.at[1]),
        pltpu.make_async_copy(og_hbm, og4, ld.at[2]),
        pltpu.make_async_copy(
            w_hbm.at[:, xcols], wfull.at[pl.ds(pl.multiple_of(h * share, 16), share), :], ld.at[3]
        ),
        pltpu.make_async_copy(q_hbm, in4.at[2], ld.at[4]),
    ]
    for copy in loads:
        copy.start()
    stores = [
        pltpu.make_async_copy(ref, dst, out.at[i])
        for i, (ref, dst) in enumerate((
            (attn_ref, attn_hbm), (dq_ref, dq_hbm), (dk_ref, dk_hbm), (dv_ref, dv_hbm),
            (gw_ref, gw_hbm)))
    ]

    barrier = pltpu.get_barrier_semaphore()
    peers = [(lax.rem(t + i, nt), h) for i in range(1, nt)]
    peers += [(t, lax.rem(h + 1, nh)), (t, lax.rem(h + nh - 1, nh)), right, left, prev2_h, next2_h]
    for peer in peers:
        pl.semaphore_signal(barrier, inc=1, device_id=peer, device_id_type=MESH)

    for i in range(2):
        loads[i].wait()
        y = in4[i].astype(F32).reshape(tokens, width)
        kvext[i, 0:tokens, :] = y.astype(BF16)
        for s, first in enumerate((0, rows - HALO)):
            parts = []
            for f in range(frames):
                a = (f * rows + first) * columns
                parts.append(y[a : a + HALO * columns])
            rsend[s, i] = jnp.concatenate(parts, axis=0).astype(BF16)

    def clear(where, first, count):
        @pl.when(jnp.logical_not(where))
        def _():
            kvext[:, first : first + count, :] = jnp.zeros((2, count, width), BF16)

    clear(before_t, early, wing)
    clear(after_t, later, wing)
    clear(before_h, up, strip)
    clear(after_h, down, strip)
    for base in (early, later):
        clear(before_h, base + side_rows, corner)
        clear(after_h, base + side_rows + corner, corner)

    def row_copies(g):
        return (
            (before_h & ~down_src, after_h, remote(
                rsend.at[0, :, :, gcols(g)], kvext.at[:, pl.ds(down, strip), gcols(g)],
                row_s.at[0, g], row_r.at[0, g], prev_h)),
            (after_h & ~up_src, before_h, remote(
                rsend.at[1, :, :, gcols(g)], kvext.at[:, pl.ds(up, strip), gcols(g)],
                row_s.at[1, g], row_r.at[1, g], next_h)),
        )

    def row_detours(g):
        return (
            (down_src, down_mid, remote(
                rsend.at[0, :, :, gcols(g)], kvpass.at[:, :, gcols(g)], kp_s.at[0, g], kp_r.at[0, g], next_h)),
            (up_src, up_mid, remote(
                rsend.at[1, :, :, gcols(g)], kvpass.at[:, :, gcols(g)], kp_s.at[0, g], kp_r.at[0, g], prev_h)),
        )

    def row_passes(g):
        return (
            (down_mid, False, remote(
                kvpass.at[:, :, gcols(g)], kvext.at[:, pl.ds(down, strip), gcols(g)], kp_s.at[1, g], row_r.at[0, g], prev2_h)),
            (up_mid, False, remote(
                kvpass.at[:, :, gcols(g)], kvext.at[:, pl.ds(up, strip), gcols(g)], kp_s.at[1, g], row_r.at[1, g], next2_h)),
        )

    def frame_copies(g):
        return (
            (before_t, after_t, remote(
                kvext.at[:, pl.ds(0, side_rows), gcols(g)],
                kvext.at[:, pl.ds(later, side_rows), gcols(g)],
                fr_s.at[0, g], fr_r.at[0, g], prev_t)),
            (after_t, before_t, remote(
                kvext.at[:, pl.ds(tokens - side_rows, side_rows), gcols(g)],
                kvext.at[:, pl.ds(early, side_rows), gcols(g)],
                fr_s.at[1, g], fr_r.at[1, g], next_t)),
        )

    def corner_copies(g):
        copies = []
        for i, (base, here) in enumerate(((up, before_h), (down, after_h))):
            shift = side_rows + i * corner
            copies.append((before_t & here, after_t & here, remote(
                kvext.at[:, pl.ds(base, corner), gcols(g)],
                kvext.at[:, pl.ds(later + shift, corner), gcols(g)],
                co_s.at[2 * i, g], co_r.at[2 * i, g], prev_t)))
            copies.append((after_t & here, before_t & here, remote(
                kvext.at[:, pl.ds(base + strip - corner, corner), gcols(g)],
                kvext.at[:, pl.ds(early + shift, corner), gcols(g)],
                co_s.at[2 * i + 1, g], co_r.at[2 * i + 1, g], next_t)))
        return copies

    def og_across(g):
        cols = pl.ds(pl.multiple_of((1 - x) * half + g * gsize, 128), gsize)
        return remote(
            ogown.at[:, cols], og2.at[pl.ds(tokens, tokens), gcols(g)],
            og_s.at[g], og_r.at[g], across)

    def begin(copies):
        for send, _, copy in copies:
            pl.when(send)(copy.start)

    def finish(copies):
        for send, recv, copy in copies:
            pl.when(send)(copy.wait_send)
            if recv is not False:
                pl.when(recv)(copy.wait_recv)

    def w_block(p, part):
        return wfull.at[pl.ds(pl.multiple_of(at(p) * share + part * cut, 16), cut), mine]

    def w_copy(i, side):
        part = i % 2 if side == 0 else 1 - i % 2
        ref = w_block(pos + (2 * side - 1) * (i // 2), part)
        return remote(ref, ref, w_s.at[side, i], w_r.at[side, i], (right, left)[side])

    def w_share(i, side):
        part = i % 2 if side == 0 else 1 - i % 2
        ref = w_block(pos + (2 * side - 1) * (i // 2 + 1), part)
        return remote(ref, ref, sh_s.at[side, i], sh_r.at[side, i], partner)

    def w_poll(i):
        for side in range(2):
            w_copy(i, side).wait()
            if i + 2 < slots:
                w_copy(i + 2, side).start()
            w_share(i, side).start()

    pl.semaphore_wait(barrier, len(peers))
    for g in range(groups):
        begin(row_detours(g))
        begin(row_copies(g))
    for g in range(groups):
        begin(frame_copies(g))
    loads[3].wait()
    for i in range(2):
        for side in range(2):
            w_copy(i, side).start()
    loads[2].wait()
    ogown[...] = og4[...].reshape(tokens, model)
    for g in range(2):
        og_across(g).start()
    piece = table_ref[:, 0:1]
    hit = jnp.ones_like(piece)
    for s, (df, dr) in enumerate(ORDER):
        a, b = t + df, h + dr
        inside = (a >= 0) & (a < nt) & (b >= 0) & (b < nh)
        here = jnp.where(inside, valid_ref[lax.rem(a + nt, nt), lax.rem(b + nh, nh)], 0)
        hit = jnp.where(piece == s + 1, here, hit)
    near = (table_ref[:, 1:2] <= reach_ref[t, 0, h]) & (table_ref[:, 2:3] <= reach_ref[t, 1, h])
    bias[...] = jnp.broadcast_to(
        jnp.where((piece == 0) | (near & (hit == 1)), 0.0, -1e30), bias.shape
    )

    loads[4].wait()
    q2[...] = in4[2].reshape(tokens, width)
    og2[0:tokens, :] = ogown[:, xcols]

    def rows_in(g):
        finish(row_detours(g))
        begin(row_passes(g))
        finish(row_copies(g))
        begin(corner_copies(g))

    rows_in(0)
    w_poll(0)
    rows_in(1)
    for g in range(2, groups):
        og_across(g).start()
    w_poll(1)

    def nt_dot(a, b):
        return lax.dot_general(a, b, (((1,), (1,)), ((), ())), preferred_element_type=F32)

    def tn_dot(a, b):
        return lax.dot_general(a, b, (((0,), (0,)), ((), ())), preferred_element_type=F32)

    def nn_dot(a, b):
        return lax.dot_general(a, b, (((1,), (0,)), ((), ())), preferred_element_type=F32)

    def head(g, j):
        return pl.ds(pl.multiple_of(g * gsize + j * HEAD_DIM, HEAD_DIM), HEAD_DIM)

    def mix_copy(g, kind):
        if kind == 0:
            return remote(
                mix.at[pl.ds(0, tokens), gcols(g)], mix.at[pl.ds(tokens, tokens), gcols(g)],
                mx_s.at[g], mx_r.at[g], across)
        first = (kind - 1) * tokens
        return remote(
            mix.at[pl.ds(first, tokens), gcols(g)],
            mix.at[pl.ds(2 * tokens + first, tokens), gcols(g)],
            mc_s.at[kind - 1, g], mc_r.at[kind - 1, g], partner)

    def forward(g):
        for j in range(gheads):
            cs = head(g, j)
            scores = nt_dot(kvext[0, :, cs], q2[:, cs]) * scale + bias[...]
            e = jnp.exp(scores - jnp.max(scores, axis=0, keepdims=True))
            p = e * (1.0 / jnp.sum(e, axis=0, keepdims=True))
            prob[g * gheads + j] = p
            mix[0:tokens, cs] = tn_dot(p.astype(BF16), kvext[1, :, cs]).astype(BF16)
        mix_copy(g, 0).start()
        mix_copy(g, 1).start()

    def forward_in(g):
        finish(frame_copies(g))
        finish(corner_copies(g))
        forward(g)

    def mix_in(g):
        mix_copy(g, 0).wait()
        mix_copy(g, 2).start()

    forward_in(0)
    rows_in(2)
    w_poll(2)
    forward_in(1)
    rows_in(3)
    w_poll(3)
    forward_in(2)
    forward_in(3)
    for g in range(groups):
        finish(row_passes(g))
    for g in range(groups):
        og_across(g).wait()
    ogc[0 : 2 * tokens, :] = og2[:, mine]
    og_core = remote(
        og2.at[:, other], ogc.at[pl.ds(2 * tokens, 2 * tokens), :],
        og_s.at[groups], og_r.at[groups], partner)
    og_core.start()
    w_poll(4)
    for g in range(groups):
        mix_in(g)
    og_core.wait()
    for g in range(groups):
        mix_copy(g, 1).wait()
        mix_copy(g, 2).wait()

    def weight(g):
        span = pl.ds(pl.multiple_of(g * gsize, 128), gsize)
        gpart[span, :] = tn_dot(mix[:, span], ogc[...])

    def gw_copy(j, side):
        return remote(
            gws.at[side, j], gwr.at[side, j], gw_s.at[side, j], gw_r.at[side, j],
            (right, left)[side])

    def gw_send(j, side):
        part = j % 2 if side == 0 else 1 - j % 2
        blk = at(pos + (1 - 2 * side) * (nh // 2 - (j + 1) // 2))
        total = gpart[pl.ds(pl.multiple_of(blk * share + part * cut, 16), cut), :]
        if j >= 2:
            total += gwr[side, j - 2].astype(F32)
        gws[side, j] = total.astype(BF16)
        gw_copy(j, side).start()

    def gw_poll(j):
        for side in range(2):
            gw_copy(j, side).wait()
            if j + 2 < slots:
                gw_send(j + 2, side)

    zfar = groups - 1 - h // 2
    weight(zfar)
    for side in range(2):
        gw_send(0, side)
    w_poll(5)

    def rest(i, carry):
        weight(lax.rem(zfar + 1 + i, groups))
        return carry

    lax.fori_loop(0, groups - 1, rest, 0)
    for side in range(2):
        gw_send(1, side)
    w_poll(6)
    for i in range(slots):
        for side in range(2):
            w_share(i, side).wait()

    def dm_copy(g):
        return remote(
            dms.at[:, gcols(g)], dmr.at[:, gcols(g)], dm_s.at[g], dm_r.at[g], across)

    def project(g, carry):
        both = nt_dot(og2[...], wfull[gcols(g), :])
        dmx[:, gcols(g)] = both[:tokens]
        dms[:, gcols(g)] = both[tokens:].astype(BF16)
        dm_copy(g).start()
        return carry

    lax.fori_loop(0, groups, project, 0)

    def attn(i, carry):
        cs = pl.ds(pl.multiple_of(i * 256, 256), 256)
        both = nn_dot(mix[0 : 2 * tokens, :], wfull[:, cs])
        attn2[:, pl.ds(pl.multiple_of(x * half + i * 256, 256), 256)] = both[:tokens].astype(BF16)
        asend[:, cs] = both[tokens:].astype(BF16)
        return carry

    gw_poll(0)
    lax.fori_loop(0, half // 256, attn, 0)
    gw_poll(1)

    def wing_copies(g):
        return (
            (before_t, after_t, remote(
                gsend.at[:, pl.ds(0, wing), gcols(g)], grecv.at[0, :, :, gcols(g)],
                g1_s.at[0, g], g1_r.at[0, g], prev_t)),
            (after_t, before_t, remote(
                gsend.at[:, pl.ds(wing, wing), gcols(g)], grecv.at[1, :, :, gcols(g)],
                g1_s.at[1, g], g1_r.at[1, g], next_t)),
        )

    def backward(g):
        dm_copy(g).wait()
        for j in range(gheads):
            cs = head(g, j)
            p = prob[g * gheads + j]
            dm = (dmx[:, cs] + dmr[:, cs].astype(F32)).astype(BF16)
            dp = nt_dot(kvext[1, :, cs], dm)
            inner = jnp.sum(p * dp, axis=0, keepdims=True)
            ds = (p * (dp - inner) * scale).astype(BF16)
            dq2[:, cs] = tn_dot(ds, kvext[0, :, cs]).astype(BF16)
            for i, grad in enumerate((nn_dot(ds, q2[:, cs]), nn_dot(p.astype(BF16), dm))):
                acc[i, :, cs] = grad[:tokens]
                gsend[i, 0:nwing, cs] = grad[tokens : tokens + nwing].astype(BF16)
                ud[i, :, cs] = grad[tokens + nwing :]
        begin(wing_copies(g))

    def strip_copies(g):
        return (
            (before_h & ~down_src, after_h, remote(
                gsend.at[:, pl.ds(nwing, strip), gcols(g)], rrecv.at[0, :, :, gcols(g)],
                g2_s.at[0, g], g2_r.at[0, g], prev_h)),
            (after_h & ~up_src, before_h, remote(
                gsend.at[:, pl.ds(nwing + strip, strip), gcols(g)], rrecv.at[1, :, :, gcols(g)],
                g2_s.at[1, g], g2_r.at[1, g], next_h)),
        )

    def strip_detours(g):
        return (
            (down_src, down_mid, remote(
                gsend.at[:, pl.ds(nwing, strip), gcols(g)], gpass.at[:, :, gcols(g)], gp_s.at[0, g], gp_r.at[0, g], next_h)),
            (up_src, up_mid, remote(
                gsend.at[:, pl.ds(nwing + strip, strip), gcols(g)], gpass.at[:, :, gcols(g)], gp_s.at[0, g], gp_r.at[0, g], prev_h)),
        )

    def strip_passes(g):
        return (
            (down_mid, False, remote(
                gpass.at[:, :, gcols(g)], rrecv.at[0, :, :, gcols(g)], gp_s.at[1, g], g2_r.at[0, g], prev2_h)),
            (up_mid, False, remote(
                gpass.at[:, :, gcols(g)], rrecv.at[1, :, :, gcols(g)], gp_s.at[1, g], g2_r.at[1, g], next2_h)),
        )

    def fold(g):
        cs = gcols(g)
        finish(wing_copies(g))
        for s, (here, tok, edge) in enumerate(
            ((after_t, tokens - side_rows, strip - corner), (before_t, 0, 0))
        ):
            @pl.when(here)
            def _():
                for i in range(2):
                    y = grecv[s, i, :, cs].astype(F32)
                    acc[i, tok : tok + side_rows, cs] += y[:side_rows]
                    ud[i, edge : edge + corner, cs] += y[side_rows : side_rows + corner]
                    ud[i, strip + edge : strip + edge + corner, cs] += y[side_rows + corner :]

        for i in range(2):
            gsend[i, nwing:, cs] = ud[i, :, cs].astype(BF16)
        begin(strip_detours(g))
        begin(strip_copies(g))

    def strips_in(g):
        finish(strip_detours(g))
        begin(strip_passes(g))

    backward(0)
    backward(1)
    gw_poll(2)
    backward(2)
    fold(0)
    backward(3)
    fold(1)
    gw_poll(3)
    fold(2)
    fold(3)
    attn_across = remote(asend, attn2.at[:, xcols], at_s.at[0], at_r.at[0], across)
    attn_across.start()
    dq_ref[...] = dq2[...].reshape(*tile, width)
    stores[1].start()
    strips_in(0)
    strips_in(1)
    gw_poll(4)
    strips_in(2)
    strips_in(3)
    gw_poll(5)
    for g in range(groups):
        finish(strip_copies(g))
        finish(strip_passes(g))
    for i, ref in enumerate((dk_ref, dv_ref)):
        for s, (here, first) in enumerate(((after_h, rows - HALO), (before_h, 0))):
            @pl.when(here)
            def _():
                y = rrecv[s, i].astype(F32)
                for f in range(frames):
                    a = (f * rows + first) * columns
                    n = HALO * columns
                    acc[i, a : a + n, :] += y[f * n : (f + 1) * n]

        ref[...] = acc[i].astype(BF16).reshape(*tile, width)
        stores[2 + i].start()
    attn_across.wait()
    attn_ref[...] = attn2[...].reshape(*tile, model)
    stores[0].start()
    gw_poll(6)
    for part in range(2):
        base = pl.multiple_of(h * share + part * cut, 16)
        gw_ref[part * cut : (part + 1) * cut, :] = (
            gpart[pl.ds(base, cut), :]
            + gwr[0, slots - 1 - part].astype(F32)
            + gwr[1, slots - 2 + part].astype(F32)
        )
    stores[4].start()
    for copy in stores:
        copy.wait()


def pass_on(*refs):
    n = len(refs) // 3
    sources, results, held, sem = refs[:n], refs[n : 2 * n], refs[2 * n : 3 * n], refs[3 * n]
    loads = [pltpu.make_async_copy(sources[i], held[i], sem.at[0, i]) for i in range(n)]
    stores = [pltpu.make_async_copy(held[i], results[i], sem.at[1, i]) for i in range(n)]
    for copy in loads:
        copy.start()
    for load, store in zip(loads, stores):
        load.wait()
        store.start()
    for store in stores:
        store.wait()


def paired(nt, nh, queries, key_tokens, value_tokens, out_weight, out_grad, window_reach, tile_valid):
    frames, rows, columns, width = queries.shape
    model = out_grad.shape[3]
    share = out_weight.shape[0]
    tokens = frames * rows * columns
    heads = width // HEAD_DIM
    halo = sum(piece_sizes(frames, rows, columns))
    strip = frames * HALO * columns
    wing = HALO * rows * columns + 2 * HALO * HALO * columns
    ext = tokens + halo
    table = np.ascontiguousarray(key_table(frames, rows, columns, ORDER).T)
    half, quarter, cut, slots = model // 2, model // 4, share // 2, nh - 1
    vmem = pl.BlockSpec(memory_space=pltpu.VMEM)
    smem = pl.BlockSpec(memory_space=pltpu.SMEM)
    hbm = pl.BlockSpec(memory_space=pl.ANY)
    dma = pltpu.SemaphoreType.DMA
    tile = (frames, rows, columns)
    shapes = (
        jax.ShapeDtypeStruct((*tile, model), BF16),
        jax.ShapeDtypeStruct((*tile, width), BF16),
        jax.ShapeDtypeStruct((*tile, width), BF16),
        jax.ShapeDtypeStruct((*tile, width), BF16),
        jax.ShapeDtypeStruct((share, quarter), F32),
    )
    results = pl.pallas_call(
        functools.partial(paired_kernel, (nt, nh, frames, rows, columns)),
        out_shape=shapes,
        in_specs=[hbm, hbm, hbm, hbm, hbm, vmem, smem, smem],
        out_specs=[hbm] * 5,
        scratch_shapes=[pltpu.VMEM(s.shape, s.dtype) for s in shapes] + [
            pltpu.VMEM((3, *tile, width), BF16),
            pltpu.VMEM((*tile, model), BF16),
            pltpu.VMEM((tokens, width), BF16),
            pltpu.VMEM((tokens, width), BF16),
            pltpu.VMEM((2, ext, width), BF16),
            pltpu.VMEM((2, 2, strip, width), BF16),
            pltpu.VMEM((width, half), BF16),
            pltpu.VMEM((tokens, model), BF16),
            pltpu.VMEM((2 * tokens, half), BF16),
            pltpu.VMEM((4 * tokens, quarter), BF16),
            pltpu.VMEM((heads, ext, tokens), F32),
            pltpu.VMEM((4 * tokens, width), BF16),
            pltpu.VMEM((tokens, width), F32),
            pltpu.VMEM((tokens, width), BF16),
            pltpu.VMEM((tokens, width), BF16),
            pltpu.VMEM((tokens, model), BF16),
            pltpu.VMEM((tokens, half), BF16),
            pltpu.VMEM((2, tokens, width), F32),
            pltpu.VMEM((2, 2 * strip, width), F32),
            pltpu.VMEM((2, halo, width), BF16),
            pltpu.VMEM((2, 2, wing, width), BF16),
            pltpu.VMEM((2, 2, strip, width), BF16),
            pltpu.VMEM((2, strip, width), BF16),
            pltpu.VMEM((2, strip, width), BF16),
            pltpu.VMEM((width, quarter), F32),
            pltpu.VMEM((2, slots, cut, quarter), BF16),
            pltpu.VMEM((2, slots, cut, quarter), BF16),
            pltpu.VMEM((ext, tokens), F32),
            dma((5,)), dma((5,)), dma((2, 4)), dma((1, 4)), dma((2, 4)), dma((1, 4)), dma((2, 4)), dma((2, 4)), dma((2, 4)), dma((2, 4)), dma((4, 4)), dma((4, 4)),
            dma((2, slots)), dma((2, slots)), dma((2, slots)), dma((2, slots)),
            dma((5,)), dma((5,)), dma((4,)), dma((4,)), dma((2, 4)), dma((2, 4)),
            dma((4,)), dma((4,)), dma((1,)), dma((1,)),
            dma((2, 4)), dma((2, 4)), dma((2, 4)), dma((2, 4)), dma((2, slots)), dma((2, slots)),
        ],
        compiler_params=pltpu.CompilerParams(
            collective_id=1, has_side_effects=True, vmem_limit_bytes=56 * 2**20
        ),
    )(
        queries, key_tokens, value_tokens, out_grad, out_weight, table,
        jnp.transpose(window_reach, (0, 2, 1)), tile_valid,
    )
    return pl.pallas_call(
        pass_on,
        out_shape=shapes,
        in_specs=[hbm] * 5,
        out_specs=[hbm] * 5,
        scratch_shapes=[pltpu.VMEM(s.shape, s.dtype) for s in shapes] + [dma((2, 5))],
    )(*results)


def solution(mesh):
    tile = P("tm", "height", None, None)
    nt, nh = mesh.shape["tm"], mesh.shape["height"]
    body = paired if (nt, nh) == (4, 8) else shards
    return jax.shard_map(
        functools.partial(body, nt, nh),
        mesh=mesh,
        in_specs=(tile, tile, tile, P("height", None), tile, P(), P()),
        out_specs=(tile, tile, tile, tile, P("height", "tm")),
        check_vma=False,
    )
```

```python
import functools
import math

import jax
import jax.numpy as jnp
import numpy as np
from jax import lax
from jax.experimental import pallas as pl
from jax.experimental.pallas import tpu as pltpu
from jax.sharding import PartitionSpec as P

HEAD_DIM = 128
HALO = 2
MESH = pl.DeviceIdType.MESH
F32 = jnp.float32
BF16 = jnp.bfloat16
SIDES = ((-1, 0), (1, 0), (0, -1), (0, 1), (-1, -1), (-1, 1), (1, -1), (1, 1))


def piece_sizes(frames, rows, columns):
    sizes = []
    for df, dr in SIDES:
        sizes.append((HALO if df else frames) * (HALO if dr else rows) * columns)
    return sizes


def key_table(frames, rows, columns, sides=SIDES):
    table = []
    for piece, (df, dr) in enumerate(((0, 0),) + sides):
        for f in range(HALO) if df else range(frames):
            for r in range(HALO) if dr else range(rows):
                fd = 0 if df == 0 else (HALO - f if df < 0 else f + 1)
                rd = 0 if dr == 0 else (HALO - r if dr < 0 else r + 1)
                table += [(piece, fd, rd)] * columns
    return np.ascontiguousarray(np.array(table, np.int32).T)


def piece_rows(df, dr, frames, rows, columns):
    fs = range(frames) if df == 0 else (range(frames - HALO, frames) if df < 0 else range(HALO))
    if dr == 0:
        return [(fs[0] * rows * columns, len(fs) * rows * columns)]
    first = (rows - HALO) if dr < 0 else 0
    return [((f * rows + first) * columns, HALO * columns) for f in fs]


def kernel(
    dims,
    q_ref, k_ref, v_ref, table_ref, reach_ref, valid_ref, w_hbm, og_hbm,
    attn_ref, dq_ref, dk_ref, dv_ref, gw_ref,
    wfull, ogown, ogcols, kvsend, kvext, gsend, grecv, prob, dmixed, mixed, mixall, acc, gpart, bias_ref, gwsend, gwrecv,
    local_sem, halo_s, halo_r, grad_s, grad_r, mix_s, mix_r,
    wr_s, wr_r, wl_s, wl_r, wc_s, wc_r, og_s, og_r, gw_s, gw_r,
):
    nt, nh, frames, rows, columns = dims
    t, h = lax.axis_index("tm"), lax.axis_index("height")
    tokens, width = q_ref.shape
    model = og_hbm.shape[1]
    share = w_hbm.shape[0]
    heads = width // HEAD_DIM
    half = model // 2
    window = gpart.shape[1]
    span_cols = model // nt
    scale = 1.0 / math.sqrt(HEAD_DIM)
    sizes = piece_sizes(frames, rows, columns)
    starts = [sum(sizes[:i]) for i in range(8)]

    def place(df, dr):
        return (lax.rem(t + nt + df, nt), lax.rem(h + nh + dr, nh))

    def exists(df, dr):
        a, b = t + df, h + dr
        return (a >= 0) & (a < nt) & (b >= 0) & (b < nh)

    def exchange(copies, sign, action):
        for (df, dr), copy in zip(SIDES, copies):
            if action == "start":
                pl.when(exists(sign * df, sign * dr))(copy.start)
            else:
                pl.when(exists(sign * df, sign * dr))(copy.wait_send)
                pl.when(exists(-sign * df, -sign * dr))(copy.wait_recv)

    def remote(src, dst, ssem, rsem, where):
        return pltpu.make_async_remote_copy(
            src_ref=src, dst_ref=dst, send_sem=ssem, recv_sem=rsem,
            device_id=where, device_id_type=MESH,
        )

    def wrow(j, lo=0, size=None):
        return pl.ds(pl.multiple_of(j * share + lo, 16), share if size is None else size)

    def orow(j, lo=0, size=None):
        return pl.ds(pl.multiple_of(j * tokens + lo, 16), tokens if size is None else size)

    own_w = pltpu.make_async_copy(w_hbm, wfull.at[wrow(h), :], local_sem.at[0])
    own_og = pltpu.make_async_copy(og_hbm, ogown, local_sem.at[1])
    own_w.start()
    own_og.start()

    barrier = pltpu.get_barrier_semaphore()
    greeted = 0
    for i in range(1, nh):
        pl.semaphore_signal(barrier, inc=1, device_id=(t, lax.rem(h + i, nh)), device_id_type=MESH)
        greeted += 1
    for i in range(1, nt):
        pl.semaphore_signal(barrier, inc=1, device_id=(lax.rem(t + i, nt), h), device_id_type=MESH)
        greeted += 1
    for df, dr in SIDES:
        if df and dr:
            pl.semaphore_signal(barrier, inc=1, device_id=place(df, dr), device_id_type=MESH)
            greeted += 1

    piece = table_ref[0:1, :]
    hit = jnp.ones_like(piece)
    for s, (df, dr) in enumerate(SIDES):
        a, b = place(df, dr)
        here = jnp.where(exists(df, dr), valid_ref[a, b], 0)
        hit = jnp.where(piece == s + 1, here, hit)
    near = (table_ref[1:2, :] <= reach_ref[t, h, 0]) & (table_ref[2:3, :] <= reach_ref[t, h, 1])
    bias_ref[...] = jnp.where((piece == 0) | (near & (hit == 1)), 0.0, -1e30)

    for i, ref in enumerate((k_ref, v_ref)):
        x = ref[...]
        kvext[i, 0:tokens, :] = x
        x = x.astype(F32)
        for s, (df, dr) in enumerate(SIDES):
            parts = [x[a : a + n] for a, n in piece_rows(df, dr, frames, rows, columns)]
            y = parts[0] if len(parts) == 1 else jnp.concatenate(parts, axis=0)
            kvsend[i, starts[s] : starts[s] + sizes[s], :] = y.astype(BF16)

    for s, (df, dr) in enumerate(SIDES):

        @pl.when(jnp.logical_not(exists(df, dr)))
        def _():
            rs = pl.ds(tokens + starts[s], sizes[s])
            kvext[:, rs, :] = jnp.zeros((2, sizes[s], width), BF16)

    par = lax.rem(h, 2)
    pos = (1 - par) * (h // 2) + par * (nh - 1 - h // 2)

    def at(p):
        p = lax.rem(p + nh, nh)
        far = p // (nh // 2)
        return (1 - far) * (2 * p) + far * (2 * (nh - 1 - p) + 1)

    right, left = (t, at(pos + 1)), (t, at(pos - 1))
    steps = nh // 2
    core = lax.rem(t, 2)
    partner = (t + 1 - 2 * core, h)
    mine = pl.ds(pl.multiple_of(core * half, 128), half)

    def span(step, size, side):
        if step < steps - 1:
            return 0, size
        return (0 if side == 0 else size // 2), size // 2

    def ring_sends(step, buf, rowfn, size, cols, sems):
        out = []
        for side, (target, sign) in enumerate(((right, -1), (left, 1))):
            lo, n = span(step, size, side)
            ref = buf.at[rowfn(at(pos + sign * step), lo, n), cols]
            ssem, rsem = sems[2 * side], sems[2 * side + 1]
            copy = remote(ref, ref, ssem.at[step], rsem.at[step], target)
            copy.start()
            out.append(copy)
        return out

    wsems = (wr_s, wr_r, wl_s, wl_r)
    def w_sends(step):
        return ring_sends(step, wfull, wrow, share, mine, wsems)

    def gw_sends(step):
        out = []
        for side, (target, sign) in enumerate(((right, 1), (left, -1))):
            base = at(pos + sign * (steps - step)) * share
            cut = share // 2
            for part in range(2):
                if step == 0 and part != side:
                    continue
                rs = slice(part * cut, (part + 1) * cut)
                total = gpart[pl.ds(pl.multiple_of(base + part * cut, 16), cut), :]
                if step > 1 or (step == 1 and part == side):
                    total += gwrecv[side, step - 1, rs, :].astype(F32)
                gwsend[side, step, rs, :] = total.astype(BF16)
            rs = pl.ds(side * cut, cut) if step == 0 else pl.ds(0, share)
            i = side * steps + step
            copy = remote(
                gwsend.at[side, step, rs, :], gwrecv.at[side, step, rs, :],
                gw_s.at[i], gw_r.at[i], target,
            )
            copy.start()
            out.append(copy)
        return out

    def cols_start(j):
        block = jnp.minimum((j * span_cols) // 128, (model - window) // 128)
        return pl.multiple_of(block * 128, 128)

    def share_sends(step):
        out = []
        for side, sign in enumerate((-1, 1)):
            lo, n = span(step, share, side)
            ref = wfull.at[wrow(at(pos + sign * (step + 1)), lo, n), mine]
            i = 2 * step + side
            out.append(remote(ref, ref, wc_s.at[i], wc_r.at[i], partner))
        for copy in out:
            copy.start()
        return out

    own_w.wait()
    own_og.wait()
    pl.semaphore_wait(barrier, greeted)
    halos = []
    for s, (df, dr) in enumerate(SIDES):
        copy = remote(
            kvsend.at[:, pl.ds(starts[s], sizes[s]), :],
            kvext.at[:, pl.ds(tokens + starts[s], sizes[s]), :],
            halo_s.at[s], halo_r.at[s], place(-df, -dr),
        )
        halos.append(copy)
    exchange(halos, -1, "start")
    live = w_sends(0)
    ogcols[orow(t), :] = ogown[:, pl.ds(cols_start(t), window)]
    gathers = []
    for i in range(1, nt):
        j = lax.rem(t + i, nt)
        copy = remote(
            ogown.at[:, pl.ds(cols_start(j), window)], ogcols.at[orow(t), :],
            og_s.at[i - 1], og_r.at[i - 1], (j, h),
        )
        copy.start()
        gathers.append(copy)
    shared = []

    def w_step(step):
        for copy in live:
            copy.wait()
        live.clear()
        if step < steps - 1:
            live.extend(w_sends(step + 1))
        shared.extend(share_sends(step))

    for step in range(2):
        w_step(step)
    exchange(halos, -1, "wait")

    group = 3 if heads % 3 == 0 else 1

    def cols_of(c):
        return pl.ds(pl.multiple_of(c * HEAD_DIM, HEAD_DIM), HEAD_DIM)

    def nt_dot(a, b):
        return lax.dot_general(a, b, (((1,), (1,)), ((), ())), preferred_element_type=F32)

    def tn_dot(a, b):
        return lax.dot_general(a, b, (((0,), (0,)), ((), ())), preferred_element_type=F32)

    def nn_dot(a, b):
        return lax.dot_general(a, b, (((1,), (0,)), ((), ())), preferred_element_type=F32)

    def forward(g, carry):
        for j in range(group):
            c = g * group + j
            cs = cols_of(c)
            scores = nt_dot(q_ref[:, cs], kvext[0, :, cs]) * scale + bias_ref[...]
            e = jnp.exp(scores - jnp.max(scores, axis=-1, keepdims=True))
            p = e / jnp.sum(e, axis=-1, keepdims=True)
            prob[c] = p
            mixed[:, cs] = nn_dot(p.astype(BF16), kvext[1, :, cs]).astype(BF16)
        return carry

    lax.fori_loop(0, heads // group, forward, 0)

    mixall[orow(t), :] = mixed[...]
    for i in range(1, nt):
        copy = remote(
            mixed, mixall.at[orow(t), :], mix_s.at[i - 1], mix_r.at[i - 1],
            (lax.rem(t + i, nt), h),
        )
        copy.start()
        gathers.append(copy)

    def gw_step(step):
        for copy in live:
            copy.wait()
        live.clear()
        if step < steps:
            live.extend(gw_sends(step))

    for step in range(2, steps):
        w_step(step)

    for copy in gathers:
        copy.wait()

    def weight(i, carry):
        cs = pl.ds(pl.multiple_of(i * 256, 256), 256)
        gpart[cs, :] = tn_dot(mixall[:, cs], ogcols[...])
        return carry

    lax.fori_loop(0, width // 256, weight, 0)
    gw_step(0)
    for copy in shared:
        copy.wait()

    def project(i, carry):
        r = pl.ds(pl.multiple_of(i * 256, 256), 256)
        dmixed[:, r] = nt_dot(ogown[...], wfull[r, :]).astype(BF16)
        return carry

    lax.fori_loop(0, width // 256, project, 0)

    gw_step(1)

    def backward(g, carry):
        for j in range(group):
            c = g * group + j
            cs = cols_of(c)
            p = prob[c]
            dm = dmixed[:, cs]
            dp = nt_dot(dm, kvext[1, :, cs])
            inner = jnp.sum(p * dp, axis=-1, keepdims=True)
            ds = (p * (dp - inner) * scale).astype(BF16)
            dq_ref[:, cs] = nn_dot(ds, kvext[0, :, cs]).astype(BF16)
            dk = tn_dot(ds, q_ref[:, cs])
            dv = tn_dot(p.astype(BF16), dm)
            acc[0, :, cs] = dk[:tokens]
            acc[1, :, cs] = dv[:tokens]
            gsend[0, :, cs] = dk[tokens:].astype(BF16)
            gsend[1, :, cs] = dv[tokens:].astype(BF16)
        return carry

    lax.fori_loop(0, heads // group, backward, 0)

    grads = []
    for s, (df, dr) in enumerate(SIDES):
        rs = pl.ds(starts[s], sizes[s])
        copy = remote(
            gsend.at[:, rs, :], grecv.at[:, rs, :], grad_s.at[s], grad_r.at[s], place(df, dr)
        )
        grads.append(copy)
    exchange(grads, 1, "start")
    gw_step(2)

    def attn(i, carry):
        cs = pl.ds(pl.multiple_of(i * 256, 256), 256)
        attn_ref[:, cs] = nn_dot(mixed[...], wfull[:, cs]).astype(BF16)
        return carry

    lax.fori_loop(0, model // 256, attn, 0)
    gw_step(3)

    exchange(grads, 1, "wait")
    for i, ref in enumerate((dk_ref, dv_ref)):
        for s, (df, dr) in enumerate(SIDES):

            @pl.when(exists(-df, -dr))
            def _():
                y = grecv[i, starts[s] : starts[s] + sizes[s], :].astype(F32)
                first = 0
                for a, n in piece_rows(df, dr, frames, rows, columns):
                    acc[i, a : a + n, :] += y[first : first + n]
                    first += n

        ref[...] = acc[i].astype(BF16)

    for step in range(4, steps + 1):
        gw_step(step)
    gw_ref[...] = (
        gpart[wrow(h), :]
        + gwrecv[0, steps - 1].astype(F32)
        + gwrecv[1, steps - 1].astype(F32)
    )


def shards(nt, nh, queries, key_tokens, value_tokens, out_weight, out_grad, window_reach, tile_valid):
    frames, rows, columns, width = queries.shape
    model = out_grad.shape[3]
    share = out_weight.shape[0]
    tokens = frames * rows * columns
    heads = width // HEAD_DIM
    halo = sum(piece_sizes(frames, rows, columns))
    ext = tokens + halo
    table = key_table(frames, rows, columns)
    narrow = (model // nt) % 128 == 0
    block = model // nt if narrow else 256
    steps = nh // 2
    vmem = pl.BlockSpec(memory_space=pltpu.VMEM)
    smem = pl.BlockSpec(memory_space=pltpu.SMEM)
    hbm = pl.BlockSpec(memory_space=pl.ANY)
    dma = pltpu.SemaphoreType.DMA
    attn, dq, dk, dv, gw = pl.pallas_call(
        functools.partial(kernel, (nt, nh, frames, rows, columns)),
        out_shape=(
            jax.ShapeDtypeStruct((tokens, model), BF16),
            jax.ShapeDtypeStruct((tokens, width), BF16),
            jax.ShapeDtypeStruct((tokens, width), BF16),
            jax.ShapeDtypeStruct((tokens, width), BF16),
            jax.ShapeDtypeStruct((share, block), F32),
        ),
        in_specs=[vmem, vmem, vmem, vmem, smem, smem, hbm, hbm],
        out_specs=[vmem] * 5,
        scratch_shapes=[
            pltpu.VMEM((width, model), BF16),
            pltpu.VMEM((tokens, model), BF16),
            pltpu.VMEM((nt * tokens, block), BF16),
            pltpu.VMEM((2, halo, width), BF16),
            pltpu.VMEM((2, ext, width), BF16),
            pltpu.VMEM((2, halo, width), BF16),
            pltpu.VMEM((2, halo, width), BF16),
            pltpu.VMEM((heads, tokens, ext), F32),
            pltpu.VMEM((tokens, width), BF16),
            pltpu.VMEM((tokens, width), BF16),
            pltpu.VMEM((nt * tokens, width), BF16),
            pltpu.VMEM((2, tokens, width), F32),
            pltpu.VMEM((width, block), F32),
            pltpu.VMEM((1, ext), F32),
            pltpu.VMEM((2, steps, share, block), BF16),
            pltpu.VMEM((2, steps, share, block), BF16),
            dma((2,)), dma((8,)), dma((8,)), dma((8,)), dma((8,)),
            dma((nt - 1,)), dma((nt - 1,)),
            dma((steps,)), dma((steps,)), dma((steps,)), dma((steps,)),
            dma((2 * steps,)), dma((2 * steps,)),
            dma((nt - 1,)), dma((nt - 1,)), dma((2 * steps,)), dma((2 * steps,)),
        ],
        compiler_params=pltpu.CompilerParams(
            collective_id=0, has_side_effects=True, vmem_limit_bytes=56 * 2**20
        ),
    )(
        queries.reshape(tokens, width),
        key_tokens.reshape(tokens, width),
        value_tokens.reshape(tokens, width),
        table,
        window_reach,
        tile_valid,
        out_weight,
        out_grad.reshape(tokens, model),
    )
    if not narrow:
        size = model // nt
        at = lax.axis_index("tm") * size
        first = jnp.minimum(at // 128, (model - block) // 128) * 128
        gw = lax.dynamic_slice_in_dim(gw, at - first, size, axis=1)
    tile = (frames, rows, columns)
    return (
        attn.reshape(*tile, model),
        dq.reshape(*tile, width),
        dk.reshape(*tile, width),
        dv.reshape(*tile, width),
        gw,
    )


ORDER = ((-1, 0), (-1, -1), (-1, 1), (1, 0), (1, -1), (1, 1), (0, -1), (0, 1))


def paired_kernel(
    dims,
    q_hbm, k_hbm, v_hbm, og_hbm, w_hbm, table_ref, reach_ref, valid_ref,
    attn_ref, dq_ref, dk_ref, dv_ref, gw_ref, in4, og4, q2, dq2, kvext, rsend, wfull, ogown, og2, ogc, prob, mix, dmx, dms, dmr, attn2, asend,
    acc, ud, gsend, grecv, rrecv, kvpass, gpass, gpart, gws, gwr, bias,
    ld, kp_s, kp_r, gp_s, gp_r, row_s, row_r, fr_s, fr_r, co_s, co_r, w_s, w_r, sh_s, sh_r, og_s, og_r, mx_s, mx_r,
    mc_s, mc_r, dm_s, dm_r, at_s, at_r, g1_s, g1_r, g2_s, g2_r, gw_s, gw_r,
):
    nt, nh, frames, rows, columns = dims
    t, h = lax.axis_index("tm"), lax.axis_index("height")
    tokens, width = q2.shape
    model = ogown.shape[1]
    share = w_hbm.shape[0]
    half, quarter = model // 2, model // 4
    cut = share // 2
    groups = 4
    gsize = width // groups
    gheads = gsize // HEAD_DIM
    tile = (frames, rows, columns)
    scale = 1.0 / math.sqrt(HEAD_DIM)
    x, core = t // 2, lax.rem(t, 2)
    partner = (t + 1 - 2 * core, h)
    across = (lax.rem(t + 2, nt), h)
    side_rows = HALO * rows * columns
    corner = HALO * HALO * columns
    strip = frames * HALO * columns
    wing = side_rows + 2 * corner
    nwing = 2 * wing
    early, later = tokens, tokens + wing
    up, down = tokens + 2 * wing, tokens + 2 * wing + strip
    before_t, after_t, before_h, after_h = t > 0, t < nt - 1, h > 0, h < nh - 1
    down_src, down_mid = h == 2, h == 3
    up_src, up_mid = h == nh - 3, h == nh - 4
    prev_t, next_t = (lax.rem(t + nt - 1, nt), h), (lax.rem(t + 1, nt), h)
    prev_h, next_h = (t, lax.rem(h + nh - 1, nh)), (t, lax.rem(h + 1, nh))
    prev2_h, next2_h = (t, lax.rem(h + nh - 2, nh)), (t, lax.rem(h + 2, nh))

    def remote(src, dst, ssem, rsem, where):
        return pltpu.make_async_remote_copy(
            src_ref=src, dst_ref=dst, send_sem=ssem, recv_sem=rsem,
            device_id=where, device_id_type=MESH,
        )

    def gcols(g):
        return pl.ds(pl.multiple_of(g * gsize, 128), gsize)

    par = lax.rem(h, 2)
    pos = (1 - par) * (h // 2) + par * (nh - 1 - h // 2)

    def at(p):
        p = lax.rem(p + nh, nh)
        far = p // (nh // 2)
        return (1 - far) * (2 * p) + far * (2 * (nh - 1 - p) + 1)

    right, left = (t, at(pos + 1)), (t, at(pos - 1))
    mine = pl.ds(pl.multiple_of(core * quarter, 128), quarter)
    other = pl.ds(pl.multiple_of((1 - core) * quarter, 128), quarter)
    xcols = pl.ds(pl.multiple_of(x * half, 128), half)
    ycols = pl.ds(pl.multiple_of((1 - x) * half, 128), half)
    slots = nh - 1
    z = h // 2
    inner = (z == 1) | (z == 2)
    turn = []
    for i, other_turn in enumerate((0, 3, 1, 2)):
        near_first = jnp.where(inner, other_turn, i)
        turn.append(jnp.where(z < 2, near_first, groups - 1 - near_first))

    loads = [
        pltpu.make_async_copy(k_hbm, in4.at[0], ld.at[0]),
        pltpu.make_async_copy(v_hbm, in4.at[1], ld.at[1]),
        pltpu.make_async_copy(og_hbm, og4, ld.at[2]),
        pltpu.make_async_copy(
            w_hbm.at[:, xcols], wfull.at[pl.ds(pl.multiple_of(h * share, 16), share), :], ld.at[3]
        ),
        pltpu.make_async_copy(q_hbm, in4.at[2], ld.at[4]),
    ]
    for copy in loads:
        copy.start()

    barrier = pltpu.get_barrier_semaphore()
    peers = [(lax.rem(t + i, nt), h) for i in range(1, nt)]
    peers += [(t, lax.rem(h + 1, nh)), (t, lax.rem(h + nh - 1, nh)), right, left, prev2_h, next2_h]
    for peer in peers:
        pl.semaphore_signal(barrier, inc=1, device_id=peer, device_id_type=MESH)

    def row_copies(g):
        return (
            (before_h & ~down_src, after_h, remote(
                rsend.at[0, :, :, gcols(g)], kvext.at[:, pl.ds(down, strip), gcols(g)],
                row_s.at[0, g], row_r.at[0, g], prev_h)),
            (after_h & ~up_src, before_h, remote(
                rsend.at[1, :, :, gcols(g)], kvext.at[:, pl.ds(up, strip), gcols(g)],
                row_s.at[1, g], row_r.at[1, g], next_h)),
        )

    def row_detours(g):
        return (
            (down_src, down_mid, remote(
                rsend.at[0, :, :, gcols(g)], kvpass.at[:, :, gcols(g)], kp_s.at[0, g], kp_r.at[0, g], next_h)),
            (up_src, up_mid, remote(
                rsend.at[1, :, :, gcols(g)], kvpass.at[:, :, gcols(g)], kp_s.at[0, g], kp_r.at[0, g], prev_h)),
        )

    def row_passes(g):
        return (
            (down_mid, False, remote(
                kvpass.at[:, :, gcols(g)], kvext.at[:, pl.ds(down, strip), gcols(g)], kp_s.at[1, g], row_r.at[0, g], prev2_h)),
            (up_mid, False, remote(
                kvpass.at[:, :, gcols(g)], kvext.at[:, pl.ds(up, strip), gcols(g)], kp_s.at[1, g], row_r.at[1, g], next2_h)),
        )

    def frame_copies(g):
        return (
            (before_t, after_t, remote(
                kvext.at[:, pl.ds(0, side_rows), gcols(g)],
                kvext.at[:, pl.ds(later, side_rows), gcols(g)],
                fr_s.at[0, g], fr_r.at[0, g], prev_t)),
            (after_t, before_t, remote(
                kvext.at[:, pl.ds(tokens - side_rows, side_rows), gcols(g)],
                kvext.at[:, pl.ds(early, side_rows), gcols(g)],
                fr_s.at[1, g], fr_r.at[1, g], next_t)),
        )

    def corner_copies(g):
        copies = []
        for i, (base, here) in enumerate(((up, before_h), (down, after_h))):
            shift = side_rows + i * corner
            copies.append((before_t & here, after_t & here, remote(
                kvext.at[:, pl.ds(base, corner), gcols(g)],
                kvext.at[:, pl.ds(later + shift, corner), gcols(g)],
                co_s.at[2 * i, g], co_r.at[2 * i, g], prev_t)))
            copies.append((after_t & here, before_t & here, remote(
                kvext.at[:, pl.ds(base + strip - corner, corner), gcols(g)],
                kvext.at[:, pl.ds(early + shift, corner), gcols(g)],
                co_s.at[2 * i + 1, g], co_r.at[2 * i + 1, g], next_t)))
        return copies

    def og_across(g):
        cols = pl.ds(pl.multiple_of((1 - x) * half + g * gsize, 128), gsize)
        return remote(
            ogown.at[:, cols], og2.at[pl.ds(tokens, tokens), gcols(g)],
            og_s.at[g], og_r.at[g], across)

    def begin(copies):
        for send, _, copy in copies:
            pl.when(send)(copy.start)

    def finish(copies):
        for send, recv, copy in copies:
            pl.when(send)(copy.wait_send)
            if recv is not False:
                pl.when(recv)(copy.wait_recv)

    def w_block(p, part):
        return wfull.at[pl.ds(pl.multiple_of(at(p) * share + part * cut, 16), cut), mine]

    def w_copy(i, side):
        part = i % 2 if side == 0 else 1 - i % 2
        ref = w_block(pos + (2 * side - 1) * (i // 2), part)
        return remote(ref, ref, w_s.at[side, i], w_r.at[side, i], (right, left)[side])

    def w_first(side):
        return remote(
            w_hbm.at[pl.ds(side * cut, cut), pl.ds(pl.multiple_of(x * half + core * quarter, 128), quarter)],
            w_block(pos, side), w_s.at[side, 0], w_r.at[side, 0], (right, left)[side])

    def w_share(i, side):
        part = i % 2 if side == 0 else 1 - i % 2
        ref = w_block(pos + (2 * side - 1) * (i // 2 + 1), part)
        return remote(ref, ref, sh_s.at[side, i], sh_r.at[side, i], partner)

    def w_poll(i):
        for side in range(2):
            w_copy(i, side).wait()
            if i + 2 < slots:
                w_copy(i + 2, side).start()
            w_share(i, side).start()

    pl.semaphore_wait(barrier, len(peers))
    for side in range(2):
        w_first(side).start()
    for i in range(2):
        loads[i].wait()
        y = in4[i].astype(F32).reshape(tokens, width)
        kvext[i, 0:tokens, :] = y.astype(BF16)
        for s, first in enumerate((0, rows - HALO)):
            parts = []
            for f in range(frames):
                a = (f * rows + first) * columns
                parts.append(y[a : a + HALO * columns])
            rsend[s, i] = jnp.concatenate(parts, axis=0).astype(BF16)

    def clear(where, first, count):
        @pl.when(jnp.logical_not(where))
        def _():
            kvext[:, first : first + count, :] = jnp.zeros((2, count, width), BF16)

    clear(before_t, early, wing)
    clear(after_t, later, wing)
    clear(before_h, up, strip)
    clear(after_h, down, strip)
    for base in (early, later):
        clear(before_h, base + side_rows, corner)
        clear(after_h, base + side_rows + corner, corner)

    for g in range(groups):
        begin(row_detours(g))
        begin(row_copies(g))
    for g in range(groups):
        begin(frame_copies(g))
    loads[3].wait()
    for side in range(2):
        w_copy(1, side).start()
    loads[2].wait()
    ogown[...] = og4[...].reshape(tokens, model)
    for g in range(2):
        og_across(g).start()
    piece = table_ref[:, 0:1]
    hit = jnp.ones_like(piece)
    for s, (df, dr) in enumerate(ORDER):
        a, b = t + df, h + dr
        inside = (a >= 0) & (a < nt) & (b >= 0) & (b < nh)
        here = jnp.where(inside, valid_ref[lax.rem(a + nt, nt), lax.rem(b + nh, nh)], 0)
        hit = jnp.where(piece == s + 1, here, hit)
    near = (table_ref[:, 1:2] <= reach_ref[t, 0, h]) & (table_ref[:, 2:3] <= reach_ref[t, 1, h])
    bias[...] = jnp.broadcast_to(
        jnp.where((piece == 0) | (near & (hit == 1)), 0.0, -1e30), bias.shape
    )

    loads[4].wait()
    q2[...] = in4[2].reshape(tokens, width)
    og2[0:tokens, :] = ogown[:, xcols]

    def rows_in(g):
        finish(row_detours(g))
        begin(row_passes(g))
        finish(row_copies(g))
        begin(corner_copies(g))

    rows_in(0)
    w_poll(0)
    rows_in(1)
    for g in range(2, groups):
        og_across(g).start()
    w_poll(1)

    def nt_dot(a, b):
        return lax.dot_general(a, b, (((1,), (1,)), ((), ())), preferred_element_type=F32)

    def tn_dot(a, b):
        return lax.dot_general(a, b, (((0,), (0,)), ((), ())), preferred_element_type=F32)

    def nn_dot(a, b):
        return lax.dot_general(a, b, (((1,), (0,)), ((), ())), preferred_element_type=F32)

    def head(g, j):
        return pl.ds(pl.multiple_of(g * gsize + j * HEAD_DIM, HEAD_DIM), HEAD_DIM)

    def mix_copy(g, kind):
        if kind == 0:
            return remote(
                mix.at[pl.ds(0, tokens), gcols(g)], mix.at[pl.ds(tokens, tokens), gcols(g)],
                mx_s.at[g], mx_r.at[g], across)
        first = (kind - 1) * tokens
        return remote(
            mix.at[pl.ds(first, tokens), gcols(g)],
            mix.at[pl.ds(2 * tokens + first, tokens), gcols(g)],
            mc_s.at[kind - 1, g], mc_r.at[kind - 1, g], partner)

    def forward(g):
        for j in range(gheads):
            cs = head(g, j)
            scores = nt_dot(kvext[0, :, cs], q2[:, cs]) * scale + bias[...]
            e = jnp.exp(scores - jnp.max(scores, axis=0, keepdims=True))
            p = e * (1.0 / jnp.sum(e, axis=0, keepdims=True))
            prob[g * gheads + j] = p
            mix[0:tokens, cs] = tn_dot(p.astype(BF16), kvext[1, :, cs]).astype(BF16)
        mix_copy(g, 0).start()
        mix_copy(g, 1).start()

    def dm_copy(i):
        cs = gcols(turn[i])
        return remote(dms.at[:, cs], dmr.at[:, cs], dm_s.at[i], dm_r.at[i], across)

    def project(i):
        cs = gcols(turn[i])
        both = nt_dot(og2[...], wfull[cs, :])
        dmx[:, cs] = both[:tokens]
        dms[:, cs] = both[tokens:].astype(BF16)
        dm_copy(i).start()

    def shares_in(first, last):
        for i in range(first, last):
            for side in range(2):
                w_share(i, side).wait()

    def forward_in(g):
        finish(frame_copies(g))
        finish(corner_copies(g))
        forward(g)

    def mix_in(g):
        mix_copy(g, 0).wait()
        mix_copy(g, 2).start()

    forward_in(0)
    rows_in(2)
    w_poll(2)
    forward_in(1)
    rows_in(3)
    w_poll(3)
    forward_in(2)
    forward_in(3)
    for g in range(groups):
        finish(row_passes(g))
    for g in range(groups):
        og_across(g).wait()
    ogc[0 : 2 * tokens, :] = og2[:, mine]
    og_core = remote(
        og2.at[:, other], ogc.at[pl.ds(2 * tokens, 2 * tokens), :],
        og_s.at[groups], og_r.at[groups], partner)
    og_core.start()
    shares_in(0, 4)
    project(0)
    w_poll(4)
    for g in range(groups):
        mix_in(g)
    og_core.wait()
    for g in range(groups):
        mix_copy(g, 1).wait()
        mix_copy(g, 2).wait()

    def weight(g):
        span = pl.ds(pl.multiple_of(g * gsize, 128), gsize)
        gpart[span, :] = tn_dot(mix[:, span], ogc[...])

    def gw_copy(j, side):
        return remote(
            gws.at[side, j], gwr.at[side, j], gw_s.at[side, j], gw_r.at[side, j],
            (right, left)[side])

    def gw_send(j, side):
        part = j % 2 if side == 0 else 1 - j % 2
        blk = at(pos + (1 - 2 * side) * (nh // 2 - (j + 1) // 2))
        total = gpart[pl.ds(pl.multiple_of(blk * share + part * cut, 16), cut), :]
        if j >= 2:
            total += gwr[side, j - 2].astype(F32)
        gws[side, j] = total.astype(BF16)
        gw_copy(j, side).start()

    def gw_poll(j):
        for side in range(2):
            gw_copy(j, side).wait()
            if j + 2 < slots:
                gw_send(j + 2, side)

    def attn(i, carry):
        cs = pl.ds(pl.multiple_of(i * 256, 256), 256)
        both = nn_dot(mix[0 : 2 * tokens, :], wfull[:, cs])
        attn2[:, pl.ds(pl.multiple_of(x * half + i * 256, 256), 256)] = both[:tokens].astype(BF16)
        asend[:, cs] = both[tokens:].astype(BF16)
        return carry

    def wing_copies(i):
        g = turn[i]
        return (
            (before_t, after_t, remote(
                gsend.at[:, pl.ds(0, wing), gcols(g)], grecv.at[0, :, :, gcols(g)],
                g1_s.at[0, i], g1_r.at[0, i], prev_t)),
            (after_t, before_t, remote(
                gsend.at[:, pl.ds(wing, wing), gcols(g)], grecv.at[1, :, :, gcols(g)],
                g1_s.at[1, i], g1_r.at[1, i], next_t)),
        )

    def attn_across(g):
        cols = pl.ds(pl.multiple_of(x * half + g * gsize, 128), gsize)
        return remote(asend.at[:, gcols(g)], attn2.at[:, cols], at_s.at[g], at_r.at[g], across)

    def backward(i):
        g = turn[i]
        dm_copy(i).wait()
        for j in range(gheads):
            cs = head(g, j)
            p = prob[g * gheads + j]
            dm = (dmx[:, cs] + dmr[:, cs].astype(F32)).astype(BF16)
            dp = nt_dot(kvext[1, :, cs], dm)
            inner = jnp.sum(p * dp, axis=0, keepdims=True)
            ds = (p * (dp - inner) * scale).astype(BF16)
            dq2[:, cs] = tn_dot(ds, kvext[0, :, cs]).astype(BF16)
            for n, grad in enumerate((nn_dot(ds, q2[:, cs]), nn_dot(p.astype(BF16), dm))):
                acc[n, :, cs] = grad[:tokens]
                gsend[n, 0:nwing, cs] = grad[tokens : tokens + nwing].astype(BF16)
                ud[n, :, cs] = grad[tokens + nwing :]
        begin(wing_copies(i))

    zfar = groups - 1 - h // 2
    weight(zfar)
    for side in range(2):
        gw_send(0, side)
    w_poll(5)

    def rest(i, carry):
        weight(lax.rem(zfar + 1 + i, groups))
        return carry

    lax.fori_loop(0, groups - 1, rest, 0)
    for side in range(2):
        gw_send(1, side)
    shares_in(4, 6)
    project(1)
    project(2)
    backward(0)
    w_poll(6)
    shares_in(6, 7)
    project(3)
    gw_poll(0)
    backward(1)
    lax.fori_loop(0, half // 256, attn, 0)
    attn_across(0).start()
    gw_poll(1)
    backward(2)
    attn_across(1).start()

    def strip_copies(g):
        return (
            (before_h & ~down_src, after_h, remote(
                gsend.at[:, pl.ds(nwing, strip), gcols(g)], rrecv.at[0, :, :, gcols(g)],
                g2_s.at[0, g], g2_r.at[0, g], prev_h)),
            (after_h & ~up_src, before_h, remote(
                gsend.at[:, pl.ds(nwing + strip, strip), gcols(g)], rrecv.at[1, :, :, gcols(g)],
                g2_s.at[1, g], g2_r.at[1, g], next_h)),
        )

    def strip_detours(g):
        return (
            (down_src, down_mid, remote(
                gsend.at[:, pl.ds(nwing, strip), gcols(g)], gpass.at[:, :, gcols(g)], gp_s.at[0, g], gp_r.at[0, g], next_h)),
            (up_src, up_mid, remote(
                gsend.at[:, pl.ds(nwing + strip, strip), gcols(g)], gpass.at[:, :, gcols(g)], gp_s.at[0, g], gp_r.at[0, g], prev_h)),
        )

    def strip_passes(g):
        return (
            (down_mid, False, remote(
                gpass.at[:, :, gcols(g)], rrecv.at[0, :, :, gcols(g)], gp_s.at[1, g], g2_r.at[0, g], prev2_h)),
            (up_mid, False, remote(
                gpass.at[:, :, gcols(g)], rrecv.at[1, :, :, gcols(g)], gp_s.at[1, g], g2_r.at[1, g], next2_h)),
        )

    def fold(i):
        g = turn[i]
        cs = gcols(g)
        finish(wing_copies(i))
        for s, (here, tok, edge) in enumerate(
            ((after_t, tokens - side_rows, strip - corner), (before_t, 0, 0))
        ):
            @pl.when(here)
            def _():
                for n in range(2):
                    y = grecv[s, n, :, cs].astype(F32)
                    acc[n, tok : tok + side_rows, cs] += y[:side_rows]
                    ud[n, edge : edge + corner, cs] += y[side_rows : side_rows + corner]
                    ud[n, strip + edge : strip + edge + corner, cs] += y[side_rows + corner :]

        for n in range(2):
            gsend[n, nwing:, cs] = ud[n, :, cs].astype(BF16)
        begin(strip_detours(g))
        begin(strip_copies(g))

    def strips_in(g):
        finish(strip_detours(g))
        begin(strip_passes(g))

    fold(0)
    gw_poll(2)
    backward(3)
    attn_across(2).start()
    attn_across(3).start()
    fold(1)
    fold(2)
    gw_poll(3)
    fold(3)
    dq_ref[...] = dq2[...].reshape(*tile, width)
    strips_in(0)
    strips_in(1)
    gw_poll(4)
    strips_in(2)
    strips_in(3)
    gw_poll(5)
    for g in range(groups):
        finish(strip_copies(g))
        finish(strip_passes(g))
    for i, ref in enumerate((dk_ref, dv_ref)):
        for s, (here, first) in enumerate(((after_h, rows - HALO), (before_h, 0))):
            @pl.when(here)
            def _():
                y = rrecv[s, i].astype(F32)
                for f in range(frames):
                    a = (f * rows + first) * columns
                    n = HALO * columns
                    acc[i, a : a + n, :] += y[f * n : (f + 1) * n]

        ref[...] = acc[i].astype(BF16).reshape(*tile, width)
    for g in range(groups):
        attn_across(g).wait()
    attn_ref[...] = attn2[...].reshape(*tile, model)
    gw_poll(6)
    for part in range(2):
        base = pl.multiple_of(h * share + part * cut, 16)
        gw_ref[part * cut : (part + 1) * cut, :] = (
            gpart[pl.ds(base, cut), :]
            + gwr[0, slots - 1 - part].astype(F32)
            + gwr[1, slots - 2 + part].astype(F32)
        )


def pass_on(*refs):
    n = len(refs) // 2
    copies = [pltpu.make_async_copy(refs[i], refs[n + i], refs[2 * n].at[i]) for i in range(n)]
    for copy in copies:
        copy.start()
    for copy in copies:
        copy.wait()


def paired(nt, nh, queries, key_tokens, value_tokens, out_weight, out_grad, window_reach, tile_valid):
    frames, rows, columns, width = queries.shape
    model = out_grad.shape[3]
    share = out_weight.shape[0]
    tokens = frames * rows * columns
    heads = width // HEAD_DIM
    halo = sum(piece_sizes(frames, rows, columns))
    strip = frames * HALO * columns
    wing = HALO * rows * columns + 2 * HALO * HALO * columns
    ext = tokens + halo
    table = np.ascontiguousarray(key_table(frames, rows, columns, ORDER).T)
    half, quarter, cut, slots = model // 2, model // 4, share // 2, nh - 1
    vmem = pl.BlockSpec(memory_space=pltpu.VMEM)
    smem = pl.BlockSpec(memory_space=pltpu.SMEM)
    hbm = pl.BlockSpec(memory_space=pl.ANY)
    dma = pltpu.SemaphoreType.DMA
    tile = (frames, rows, columns)
    shapes = (
        jax.ShapeDtypeStruct((*tile, model), BF16),
        jax.ShapeDtypeStruct((*tile, width), BF16),
        jax.ShapeDtypeStruct((*tile, width), BF16),
        jax.ShapeDtypeStruct((*tile, width), BF16),
        jax.ShapeDtypeStruct((share, quarter), F32),
    )
    results = pl.pallas_call(
        functools.partial(paired_kernel, (nt, nh, frames, rows, columns)),
        out_shape=[pltpu.VMEM(s.shape, s.dtype) for s in shapes],
        in_specs=[hbm, hbm, hbm, hbm, hbm, vmem, smem, smem],
        out_specs=[vmem] * 5,
        scratch_shapes=[
            pltpu.VMEM((3, *tile, width), BF16),
            pltpu.VMEM((*tile, model), BF16),
            pltpu.VMEM((tokens, width), BF16),
            pltpu.VMEM((tokens, width), BF16),
            pltpu.VMEM((2, ext, width), BF16),
            pltpu.VMEM((2, 2, strip, width), BF16),
            pltpu.VMEM((width, half), BF16),
            pltpu.VMEM((tokens, model), BF16),
            pltpu.VMEM((2 * tokens, half), BF16),
            pltpu.VMEM((4 * tokens, quarter), BF16),
            pltpu.VMEM((heads, ext, tokens), F32),
            pltpu.VMEM((4 * tokens, width), BF16),
            pltpu.VMEM((tokens, width), F32),
            pltpu.VMEM((tokens, width), BF16),
            pltpu.VMEM((tokens, width), BF16),
            pltpu.VMEM((tokens, model), BF16),
            pltpu.VMEM((tokens, half), BF16),
            pltpu.VMEM((2, tokens, width), F32),
            pltpu.VMEM((2, 2 * strip, width), F32),
            pltpu.VMEM((2, halo, width), BF16),
            pltpu.VMEM((2, 2, wing, width), BF16),
            pltpu.VMEM((2, 2, strip, width), BF16),
            pltpu.VMEM((2, strip, width), BF16),
            pltpu.VMEM((2, strip, width), BF16),
            pltpu.VMEM((width, quarter), F32),
            pltpu.VMEM((2, slots, cut, quarter), BF16),
            pltpu.VMEM((2, slots, cut, quarter), BF16),
            pltpu.VMEM((ext, tokens), F32),
            dma((5,)), dma((2, 4)), dma((1, 4)), dma((2, 4)), dma((1, 4)), dma((2, 4)), dma((2, 4)), dma((2, 4)), dma((2, 4)), dma((4, 4)), dma((4, 4)),
            dma((2, slots)), dma((2, slots)), dma((2, slots)), dma((2, slots)),
            dma((5,)), dma((5,)), dma((4,)), dma((4,)), dma((2, 4)), dma((2, 4)),
            dma((4,)), dma((4,)), dma((4,)), dma((4,)),
            dma((2, 4)), dma((2, 4)), dma((2, 4)), dma((2, 4)), dma((2, slots)), dma((2, slots)),
        ],
        compiler_params=pltpu.CompilerParams(
            collective_id=1, has_side_effects=True, vmem_limit_bytes=56 * 2**20
        ),
    )(
        queries, key_tokens, value_tokens, out_grad, out_weight, table,
        jnp.transpose(window_reach, (0, 2, 1)), tile_valid,
    )
    return pl.pallas_call(
        pass_on,
        out_shape=shapes,
        in_specs=[vmem] * 5,
        out_specs=[hbm] * 5,
        scratch_shapes=[dma((5,))],
    )(*[pltpu.with_memory_space_constraint(r, pltpu.VMEM) for r in results])


def solution(mesh):
    tile = P("tm", "height", None, None)
    nt, nh = mesh.shape["tm"], mesh.shape["height"]
    body = paired if (nt, nh) == (4, 8) else shards
    return jax.shard_map(
        functools.partial(body, nt, nh),
        mesh=mesh,
        in_specs=(tile, tile, tile, P("height", None), tile, P(), P()),
        out_specs=(tile, tile, tile, tile, P("height", "tm")),
        check_vma=False,
    )
```

```python
import functools
import math

import jax
import jax.numpy as jnp
import numpy as np
from jax import lax
from jax.experimental import pallas as pl
from jax.experimental.pallas import tpu as pltpu
from jax.sharding import PartitionSpec as P

HEAD_DIM = 128
HALO = 2
MESH = pl.DeviceIdType.MESH
F32 = jnp.float32
BF16 = jnp.bfloat16
SIDES = ((-1, 0), (1, 0), (0, -1), (0, 1), (-1, -1), (-1, 1), (1, -1), (1, 1))


def piece_sizes(frames, rows, columns):
    sizes = []
    for df, dr in SIDES:
        sizes.append((HALO if df else frames) * (HALO if dr else rows) * columns)
    return sizes


def key_table(frames, rows, columns, sides=SIDES):
    table = []
    for piece, (df, dr) in enumerate(((0, 0),) + sides):
        for f in range(HALO) if df else range(frames):
            for r in range(HALO) if dr else range(rows):
                fd = 0 if df == 0 else (HALO - f if df < 0 else f + 1)
                rd = 0 if dr == 0 else (HALO - r if dr < 0 else r + 1)
                table += [(piece, fd, rd)] * columns
    return np.ascontiguousarray(np.array(table, np.int32).T)


def piece_rows(df, dr, frames, rows, columns):
    fs = range(frames) if df == 0 else (range(frames - HALO, frames) if df < 0 else range(HALO))
    if dr == 0:
        return [(fs[0] * rows * columns, len(fs) * rows * columns)]
    first = (rows - HALO) if dr < 0 else 0
    return [((f * rows + first) * columns, HALO * columns) for f in fs]


def kernel(
    dims,
    q_ref, k_ref, v_ref, table_ref, reach_ref, valid_ref, w_hbm, og_hbm,
    attn_ref, dq_ref, dk_ref, dv_ref, gw_ref,
    wfull, ogown, ogcols, kvsend, kvext, gsend, grecv, prob, dmixed, mixed, mixall, acc, gpart, bias_ref, gwsend, gwrecv,
    local_sem, halo_s, halo_r, grad_s, grad_r, mix_s, mix_r,
    wr_s, wr_r, wl_s, wl_r, wc_s, wc_r, og_s, og_r, gw_s, gw_r,
):
    nt, nh, frames, rows, columns = dims
    t, h = lax.axis_index("tm"), lax.axis_index("height")
    tokens, width = q_ref.shape
    model = og_hbm.shape[1]
    share = w_hbm.shape[0]
    heads = width // HEAD_DIM
    half = model // 2
    window = gpart.shape[1]
    span_cols = model // nt
    scale = 1.0 / math.sqrt(HEAD_DIM)
    sizes = piece_sizes(frames, rows, columns)
    starts = [sum(sizes[:i]) for i in range(8)]

    def place(df, dr):
        return (lax.rem(t + nt + df, nt), lax.rem(h + nh + dr, nh))

    def exists(df, dr):
        a, b = t + df, h + dr
        return (a >= 0) & (a < nt) & (b >= 0) & (b < nh)

    def exchange(copies, sign, action):
        for (df, dr), copy in zip(SIDES, copies):
            if action == "start":
                pl.when(exists(sign * df, sign * dr))(copy.start)
            else:
                pl.when(exists(sign * df, sign * dr))(copy.wait_send)
                pl.when(exists(-sign * df, -sign * dr))(copy.wait_recv)

    def remote(src, dst, ssem, rsem, where):
        return pltpu.make_async_remote_copy(
            src_ref=src, dst_ref=dst, send_sem=ssem, recv_sem=rsem,
            device_id=where, device_id_type=MESH,
        )

    def wrow(j, lo=0, size=None):
        return pl.ds(pl.multiple_of(j * share + lo, 16), share if size is None else size)

    def orow(j, lo=0, size=None):
        return pl.ds(pl.multiple_of(j * tokens + lo, 16), tokens if size is None else size)

    own_w = pltpu.make_async_copy(w_hbm, wfull.at[wrow(h), :], local_sem.at[0])
    own_og = pltpu.make_async_copy(og_hbm, ogown, local_sem.at[1])
    own_w.start()
    own_og.start()

    barrier = pltpu.get_barrier_semaphore()
    greeted = 0
    for i in range(1, nh):
        pl.semaphore_signal(barrier, inc=1, device_id=(t, lax.rem(h + i, nh)), device_id_type=MESH)
        greeted += 1
    for i in range(1, nt):
        pl.semaphore_signal(barrier, inc=1, device_id=(lax.rem(t + i, nt), h), device_id_type=MESH)
        greeted += 1
    for df, dr in SIDES:
        if df and dr:
            pl.semaphore_signal(barrier, inc=1, device_id=place(df, dr), device_id_type=MESH)
            greeted += 1

    piece = table_ref[0:1, :]
    hit = jnp.ones_like(piece)
    for s, (df, dr) in enumerate(SIDES):
        a, b = place(df, dr)
        here = jnp.where(exists(df, dr), valid_ref[a, b], 0)
        hit = jnp.where(piece == s + 1, here, hit)
    near = (table_ref[1:2, :] <= reach_ref[t, h, 0]) & (table_ref[2:3, :] <= reach_ref[t, h, 1])
    bias_ref[...] = jnp.where((piece == 0) | (near & (hit == 1)), 0.0, -1e30)

    for i, ref in enumerate((k_ref, v_ref)):
        x = ref[...]
        kvext[i, 0:tokens, :] = x
        x = x.astype(F32)
        for s, (df, dr) in enumerate(SIDES):
            parts = [x[a : a + n] for a, n in piece_rows(df, dr, frames, rows, columns)]
            y = parts[0] if len(parts) == 1 else jnp.concatenate(parts, axis=0)
            kvsend[i, starts[s] : starts[s] + sizes[s], :] = y.astype(BF16)

    for s, (df, dr) in enumerate(SIDES):

        @pl.when(jnp.logical_not(exists(df, dr)))
        def _():
            rs = pl.ds(tokens + starts[s], sizes[s])
            kvext[:, rs, :] = jnp.zeros((2, sizes[s], width), BF16)

    par = lax.rem(h, 2)
    pos = (1 - par) * (h // 2) + par * (nh - 1 - h // 2)

    def at(p):
        p = lax.rem(p + nh, nh)
        far = p // (nh // 2)
        return (1 - far) * (2 * p) + far * (2 * (nh - 1 - p) + 1)

    right, left = (t, at(pos + 1)), (t, at(pos - 1))
    steps = nh // 2
    core = lax.rem(t, 2)
    partner = (t + 1 - 2 * core, h)
    mine = pl.ds(pl.multiple_of(core * half, 128), half)

    def span(step, size, side):
        if step < steps - 1:
            return 0, size
        return (0 if side == 0 else size // 2), size // 2

    def ring_sends(step, buf, rowfn, size, cols, sems):
        out = []
        for side, (target, sign) in enumerate(((right, -1), (left, 1))):
            lo, n = span(step, size, side)
            ref = buf.at[rowfn(at(pos + sign * step), lo, n), cols]
            ssem, rsem = sems[2 * side], sems[2 * side + 1]
            copy = remote(ref, ref, ssem.at[step], rsem.at[step], target)
            copy.start()
            out.append(copy)
        return out

    wsems = (wr_s, wr_r, wl_s, wl_r)
    def w_sends(step):
        return ring_sends(step, wfull, wrow, share, mine, wsems)

    def gw_sends(step):
        out = []
        for side, (target, sign) in enumerate(((right, 1), (left, -1))):
            base = at(pos + sign * (steps - step)) * share
            cut = share // 2
            for part in range(2):
                if step == 0 and part != side:
                    continue
                rs = slice(part * cut, (part + 1) * cut)
                total = gpart[pl.ds(pl.multiple_of(base + part * cut, 16), cut), :]
                if step > 1 or (step == 1 and part == side):
                    total += gwrecv[side, step - 1, rs, :].astype(F32)
                gwsend[side, step, rs, :] = total.astype(BF16)
            rs = pl.ds(side * cut, cut) if step == 0 else pl.ds(0, share)
            i = side * steps + step
            copy = remote(
                gwsend.at[side, step, rs, :], gwrecv.at[side, step, rs, :],
                gw_s.at[i], gw_r.at[i], target,
            )
            copy.start()
            out.append(copy)
        return out

    def cols_start(j):
        block = jnp.minimum((j * span_cols) // 128, (model - window) // 128)
        return pl.multiple_of(block * 128, 128)

    def share_sends(step):
        out = []
        for side, sign in enumerate((-1, 1)):
            lo, n = span(step, share, side)
            ref = wfull.at[wrow(at(pos + sign * (step + 1)), lo, n), mine]
            i = 2 * step + side
            out.append(remote(ref, ref, wc_s.at[i], wc_r.at[i], partner))
        for copy in out:
            copy.start()
        return out

    own_w.wait()
    own_og.wait()
    pl.semaphore_wait(barrier, greeted)
    halos = []
    for s, (df, dr) in enumerate(SIDES):
        copy = remote(
            kvsend.at[:, pl.ds(starts[s], sizes[s]), :],
            kvext.at[:, pl.ds(tokens + starts[s], sizes[s]), :],
            halo_s.at[s], halo_r.at[s], place(-df, -dr),
        )
        halos.append(copy)
    exchange(halos, -1, "start")
    live = w_sends(0)
    ogcols[orow(t), :] = ogown[:, pl.ds(cols_start(t), window)]
    gathers = []
    for i in range(1, nt):
        j = lax.rem(t + i, nt)
        copy = remote(
            ogown.at[:, pl.ds(cols_start(j), window)], ogcols.at[orow(t), :],
            og_s.at[i - 1], og_r.at[i - 1], (j, h),
        )
        copy.start()
        gathers.append(copy)
    shared = []

    def w_step(step):
        for copy in live:
            copy.wait()
        live.clear()
        if step < steps - 1:
            live.extend(w_sends(step + 1))
        shared.extend(share_sends(step))

    for step in range(2):
        w_step(step)
    exchange(halos, -1, "wait")

    group = 3 if heads % 3 == 0 else 1

    def cols_of(c):
        return pl.ds(pl.multiple_of(c * HEAD_DIM, HEAD_DIM), HEAD_DIM)

    def nt_dot(a, b):
        return lax.dot_general(a, b, (((1,), (1,)), ((), ())), preferred_element_type=F32)

    def tn_dot(a, b):
        return lax.dot_general(a, b, (((0,), (0,)), ((), ())), preferred_element_type=F32)

    def nn_dot(a, b):
        return lax.dot_general(a, b, (((1,), (0,)), ((), ())), preferred_element_type=F32)

    def forward(g, carry):
        for j in range(group):
            c = g * group + j
            cs = cols_of(c)
            scores = nt_dot(q_ref[:, cs], kvext[0, :, cs]) * scale + bias_ref[...]
            e = jnp.exp(scores - jnp.max(scores, axis=-1, keepdims=True))
            p = e / jnp.sum(e, axis=-1, keepdims=True)
            prob[c] = p
            mixed[:, cs] = nn_dot(p.astype(BF16), kvext[1, :, cs]).astype(BF16)
        return carry

    lax.fori_loop(0, heads // group, forward, 0)

    mixall[orow(t), :] = mixed[...]
    for i in range(1, nt):
        copy = remote(
            mixed, mixall.at[orow(t), :], mix_s.at[i - 1], mix_r.at[i - 1],
            (lax.rem(t + i, nt), h),
        )
        copy.start()
        gathers.append(copy)

    def gw_step(step):
        for copy in live:
            copy.wait()
        live.clear()
        if step < steps:
            live.extend(gw_sends(step))

    for step in range(2, steps):
        w_step(step)

    for copy in gathers:
        copy.wait()

    def weight(i, carry):
        cs = pl.ds(pl.multiple_of(i * 256, 256), 256)
        gpart[cs, :] = tn_dot(mixall[:, cs], ogcols[...])
        return carry

    lax.fori_loop(0, width // 256, weight, 0)
    gw_step(0)
    for copy in shared:
        copy.wait()

    def project(i, carry):
        r = pl.ds(pl.multiple_of(i * 256, 256), 256)
        dmixed[:, r] = nt_dot(ogown[...], wfull[r, :]).astype(BF16)
        return carry

    lax.fori_loop(0, width // 256, project, 0)

    gw_step(1)

    def backward(g, carry):
        for j in range(group):
            c = g * group + j
            cs = cols_of(c)
            p = prob[c]
            dm = dmixed[:, cs]
            dp = nt_dot(dm, kvext[1, :, cs])
            inner = jnp.sum(p * dp, axis=-1, keepdims=True)
            ds = (p * (dp - inner) * scale).astype(BF16)
            dq_ref[:, cs] = nn_dot(ds, kvext[0, :, cs]).astype(BF16)
            dk = tn_dot(ds, q_ref[:, cs])
            dv = tn_dot(p.astype(BF16), dm)
            acc[0, :, cs] = dk[:tokens]
            acc[1, :, cs] = dv[:tokens]
            gsend[0, :, cs] = dk[tokens:].astype(BF16)
            gsend[1, :, cs] = dv[tokens:].astype(BF16)
        return carry

    lax.fori_loop(0, heads // group, backward, 0)

    grads = []
    for s, (df, dr) in enumerate(SIDES):
        rs = pl.ds(starts[s], sizes[s])
        copy = remote(
            gsend.at[:, rs, :], grecv.at[:, rs, :], grad_s.at[s], grad_r.at[s], place(df, dr)
        )
        grads.append(copy)
    exchange(grads, 1, "start")
    gw_step(2)

    def attn(i, carry):
        cs = pl.ds(pl.multiple_of(i * 256, 256), 256)
        attn_ref[:, cs] = nn_dot(mixed[...], wfull[:, cs]).astype(BF16)
        return carry

    lax.fori_loop(0, model // 256, attn, 0)
    gw_step(3)

    exchange(grads, 1, "wait")
    for i, ref in enumerate((dk_ref, dv_ref)):
        for s, (df, dr) in enumerate(SIDES):

            @pl.when(exists(-df, -dr))
            def _():
                y = grecv[i, starts[s] : starts[s] + sizes[s], :].astype(F32)
                first = 0
                for a, n in piece_rows(df, dr, frames, rows, columns):
                    acc[i, a : a + n, :] += y[first : first + n]
                    first += n

        ref[...] = acc[i].astype(BF16)

    for step in range(4, steps + 1):
        gw_step(step)
    gw_ref[...] = (
        gpart[wrow(h), :]
        + gwrecv[0, steps - 1].astype(F32)
        + gwrecv[1, steps - 1].astype(F32)
    )


def shards(nt, nh, queries, key_tokens, value_tokens, out_weight, out_grad, window_reach, tile_valid):
    frames, rows, columns, width = queries.shape
    model = out_grad.shape[3]
    share = out_weight.shape[0]
    tokens = frames * rows * columns
    heads = width // HEAD_DIM
    halo = sum(piece_sizes(frames, rows, columns))
    ext = tokens + halo
    table = key_table(frames, rows, columns)
    narrow = (model // nt) % 128 == 0
    block = model // nt if narrow else 256
    steps = nh // 2
    vmem = pl.BlockSpec(memory_space=pltpu.VMEM)
    smem = pl.BlockSpec(memory_space=pltpu.SMEM)
    hbm = pl.BlockSpec(memory_space=pl.ANY)
    dma = pltpu.SemaphoreType.DMA
    attn, dq, dk, dv, gw = pl.pallas_call(
        functools.partial(kernel, (nt, nh, frames, rows, columns)),
        out_shape=(
            jax.ShapeDtypeStruct((tokens, model), BF16),
            jax.ShapeDtypeStruct((tokens, width), BF16),
            jax.ShapeDtypeStruct((tokens, width), BF16),
            jax.ShapeDtypeStruct((tokens, width), BF16),
            jax.ShapeDtypeStruct((share, block), F32),
        ),
        in_specs=[vmem, vmem, vmem, vmem, smem, smem, hbm, hbm],
        out_specs=[vmem] * 5,
        scratch_shapes=[
            pltpu.VMEM((width, model), BF16),
            pltpu.VMEM((tokens, model), BF16),
            pltpu.VMEM((nt * tokens, block), BF16),
            pltpu.VMEM((2, halo, width), BF16),
            pltpu.VMEM((2, ext, width), BF16),
            pltpu.VMEM((2, halo, width), BF16),
            pltpu.VMEM((2, halo, width), BF16),
            pltpu.VMEM((heads, tokens, ext), F32),
            pltpu.VMEM((tokens, width), BF16),
            pltpu.VMEM((tokens, width), BF16),
            pltpu.VMEM((nt * tokens, width), BF16),
            pltpu.VMEM((2, tokens, width), F32),
            pltpu.VMEM((width, block), F32),
            pltpu.VMEM((1, ext), F32),
            pltpu.VMEM((2, steps, share, block), BF16),
            pltpu.VMEM((2, steps, share, block), BF16),
            dma((2,)), dma((8,)), dma((8,)), dma((8,)), dma((8,)),
            dma((nt - 1,)), dma((nt - 1,)),
            dma((steps,)), dma((steps,)), dma((steps,)), dma((steps,)),
            dma((2 * steps,)), dma((2 * steps,)),
            dma((nt - 1,)), dma((nt - 1,)), dma((2 * steps,)), dma((2 * steps,)),
        ],
        compiler_params=pltpu.CompilerParams(
            collective_id=0, has_side_effects=True, vmem_limit_bytes=56 * 2**20
        ),
    )(
        queries.reshape(tokens, width),
        key_tokens.reshape(tokens, width),
        value_tokens.reshape(tokens, width),
        table,
        window_reach,
        tile_valid,
        out_weight,
        out_grad.reshape(tokens, model),
    )
    if not narrow:
        size = model // nt
        at = lax.axis_index("tm") * size
        first = jnp.minimum(at // 128, (model - block) // 128) * 128
        gw = lax.dynamic_slice_in_dim(gw, at - first, size, axis=1)
    tile = (frames, rows, columns)
    return (
        attn.reshape(*tile, model),
        dq.reshape(*tile, width),
        dk.reshape(*tile, width),
        dv.reshape(*tile, width),
        gw,
    )


ORDER = ((-1, 0), (-1, -1), (-1, 1), (1, 0), (1, -1), (1, 1), (0, -1), (0, 1))


def paired_kernel(
    dims,
    q_hbm, k_hbm, v_hbm, og_hbm, w_hbm, table_ref, reach_ref, valid_ref,
    attn_ref, dq_ref, dk_ref, dv_ref, gw_ref, in4, og4, q2, dq2, kvext, rsend, wfull, ogown, og2, ogc, prob, mix, dmx, dms, dmr, attn2, asend,
    acc, ud, gsend, grecv, rrecv, kvpass, gpass, gpart, gws, gwr, bias,
    ld, kp_s, kp_r, gp_s, gp_r, row_s, row_r, fr_s, fr_r, co_s, co_r, w_s, w_r, sh_s, sh_r, og_s, og_r, mx_s, mx_r,
    mc_s, mc_r, dm_s, dm_r, at_s, at_r, g1_s, g1_r, g2_s, g2_r, gw_s, gw_r,
):
    nt, nh, frames, rows, columns = dims
    t, h = lax.axis_index("tm"), lax.axis_index("height")
    tokens, width = q2.shape
    model = ogown.shape[1]
    share = w_hbm.shape[0]
    half, quarter = model // 2, model // 4
    cut = share // 2
    groups = 4
    gsize = width // groups
    gheads = gsize // HEAD_DIM
    tile = (frames, rows, columns)
    scale = 1.0 / math.sqrt(HEAD_DIM)
    x, core = t // 2, lax.rem(t, 2)
    partner = (t + 1 - 2 * core, h)
    across = (lax.rem(t + 2, nt), h)
    side_rows = HALO * rows * columns
    corner = HALO * HALO * columns
    strip = frames * HALO * columns
    wing = side_rows + 2 * corner
    nwing = 2 * wing
    early, later = tokens, tokens + wing
    up, down = tokens + 2 * wing, tokens + 2 * wing + strip
    before_t, after_t, before_h, after_h = t > 0, t < nt - 1, h > 0, h < nh - 1
    down_src, down_mid = h == 2, h == 3
    up_src, up_mid = h == nh - 3, h == nh - 4
    prev_t, next_t = (lax.rem(t + nt - 1, nt), h), (lax.rem(t + 1, nt), h)
    prev_h, next_h = (t, lax.rem(h + nh - 1, nh)), (t, lax.rem(h + 1, nh))
    prev2_h, next2_h = (t, lax.rem(h + nh - 2, nh)), (t, lax.rem(h + 2, nh))

    def remote(src, dst, ssem, rsem, where):
        return pltpu.make_async_remote_copy(
            src_ref=src, dst_ref=dst, send_sem=ssem, recv_sem=rsem,
            device_id=where, device_id_type=MESH,
        )

    def gcols(g):
        return pl.ds(pl.multiple_of(g * gsize, 128), gsize)

    par = lax.rem(h, 2)
    pos = (1 - par) * (h // 2) + par * (nh - 1 - h // 2)

    def at(p):
        p = lax.rem(p + nh, nh)
        far = p // (nh // 2)
        return (1 - far) * (2 * p) + far * (2 * (nh - 1 - p) + 1)

    right, left = (t, at(pos + 1)), (t, at(pos - 1))
    mine = pl.ds(pl.multiple_of(core * quarter, 128), quarter)
    other = pl.ds(pl.multiple_of((1 - core) * quarter, 128), quarter)
    xcols = pl.ds(pl.multiple_of(x * half, 128), half)
    ycols = pl.ds(pl.multiple_of((1 - x) * half, 128), half)
    slots = nh - 1
    z = h // 2
    inner = (z == 1) | (z == 2)
    turn = []
    for i, other_turn in enumerate((0, 3, 1, 2)):
        near_first = jnp.where(inner, other_turn, i)
        turn.append(jnp.where(z < 2, near_first, groups - 1 - near_first))

    loads = [
        pltpu.make_async_copy(k_hbm, in4.at[0], ld.at[0]),
        pltpu.make_async_copy(v_hbm, in4.at[1], ld.at[1]),
        pltpu.make_async_copy(og_hbm, og4, ld.at[2]),
        pltpu.make_async_copy(
            w_hbm.at[:, xcols], wfull.at[pl.ds(pl.multiple_of(h * share, 16), share), :], ld.at[3]
        ),
        pltpu.make_async_copy(q_hbm, in4.at[2], ld.at[4]),
    ]
    barrier = pltpu.get_barrier_semaphore()
    peers = [(lax.rem(t + i, nt), h) for i in range(1, nt)]
    peers += [(t, lax.rem(h + 1, nh)), (t, lax.rem(h + nh - 1, nh)), right, left, prev2_h, next2_h]
    for peer in peers:
        pl.semaphore_signal(barrier, inc=1, device_id=peer, device_id_type=MESH)
    for copy in loads:
        copy.start()


    def row_copies(g):
        return (
            (before_h & ~down_src, after_h, remote(
                rsend.at[0, :, :, gcols(g)], kvext.at[:, pl.ds(down, strip), gcols(g)],
                row_s.at[0, g], row_r.at[0, g], prev_h)),
            (after_h & ~up_src, before_h, remote(
                rsend.at[1, :, :, gcols(g)], kvext.at[:, pl.ds(up, strip), gcols(g)],
                row_s.at[1, g], row_r.at[1, g], next_h)),
        )

    def row_detours(g):
        return (
            (down_src, down_mid, remote(
                rsend.at[0, :, :, gcols(g)], kvpass.at[:, :, gcols(g)], kp_s.at[0, g], kp_r.at[0, g], next_h)),
            (up_src, up_mid, remote(
                rsend.at[1, :, :, gcols(g)], kvpass.at[:, :, gcols(g)], kp_s.at[0, g], kp_r.at[0, g], prev_h)),
        )

    def row_passes(g):
        return (
            (down_mid, False, remote(
                kvpass.at[:, :, gcols(g)], kvext.at[:, pl.ds(down, strip), gcols(g)], kp_s.at[1, g], row_r.at[0, g], prev2_h)),
            (up_mid, False, remote(
                kvpass.at[:, :, gcols(g)], kvext.at[:, pl.ds(up, strip), gcols(g)], kp_s.at[1, g], row_r.at[1, g], next2_h)),
        )

    def frame_copies(g):
        return (
            (before_t, after_t, remote(
                kvext.at[:, pl.ds(0, side_rows), gcols(g)],
                kvext.at[:, pl.ds(later, side_rows), gcols(g)],
                fr_s.at[0, g], fr_r.at[0, g], prev_t)),
            (after_t, before_t, remote(
                kvext.at[:, pl.ds(tokens - side_rows, side_rows), gcols(g)],
                kvext.at[:, pl.ds(early, side_rows), gcols(g)],
                fr_s.at[1, g], fr_r.at[1, g], next_t)),
        )

    def corner_copies(g):
        copies = []
        for i, (base, here) in enumerate(((up, before_h), (down, after_h))):
            shift = side_rows + i * corner
            copies.append((before_t & here, after_t & here, remote(
                kvext.at[:, pl.ds(base, corner), gcols(g)],
                kvext.at[:, pl.ds(later + shift, corner), gcols(g)],
                co_s.at[2 * i, g], co_r.at[2 * i, g], prev_t)))
            copies.append((after_t & here, before_t & here, remote(
                kvext.at[:, pl.ds(base + strip - corner, corner), gcols(g)],
                kvext.at[:, pl.ds(early + shift, corner), gcols(g)],
                co_s.at[2 * i + 1, g], co_r.at[2 * i + 1, g], next_t)))
        return copies

    def og_across(g):
        cols = pl.ds(pl.multiple_of((1 - x) * half + g * gsize, 128), gsize)
        return remote(
            ogown.at[:, cols], og2.at[pl.ds(tokens, tokens), gcols(g)],
            og_s.at[g], og_r.at[g], across)

    def begin(copies):
        for send, _, copy in copies:
            pl.when(send)(copy.start)

    def finish(copies):
        for send, recv, copy in copies:
            pl.when(send)(copy.wait_send)
            if recv is not False:
                pl.when(recv)(copy.wait_recv)

    def w_block(p, part):
        return wfull.at[pl.ds(pl.multiple_of(at(p) * share + part * cut, 16), cut), mine]

    def w_copy(i, side):
        part = i % 2 if side == 0 else 1 - i % 2
        ref = w_block(pos + (2 * side - 1) * (i // 2), part)
        return remote(ref, ref, w_s.at[side, i], w_r.at[side, i], (right, left)[side])

    def w_first(side):
        return remote(
            w_hbm.at[pl.ds(side * cut, cut), pl.ds(pl.multiple_of(x * half + core * quarter, 128), quarter)],
            w_block(pos, side), w_s.at[side, 0], w_r.at[side, 0], (right, left)[side])

    def w_share(i, side):
        part = i % 2 if side == 0 else 1 - i % 2
        ref = w_block(pos + (2 * side - 1) * (i // 2 + 1), part)
        return remote(ref, ref, sh_s.at[side, i], sh_r.at[side, i], partner)

    def w_poll(i):
        for side in range(2):
            w_copy(i, side).wait()
            if i + 2 < slots:
                w_copy(i + 2, side).start()
            w_share(i, side).start()

    pl.semaphore_wait(barrier, len(peers))
    for side in range(2):
        w_first(side).start()
    for i in range(2):
        loads[i].wait()
        y = in4[i].astype(F32).reshape(tokens, width)
        kvext[i, 0:tokens, :] = y.astype(BF16)
        for s, first in enumerate((0, rows - HALO)):
            parts = []
            for f in range(frames):
                a = (f * rows + first) * columns
                parts.append(y[a : a + HALO * columns])
            rsend[s, i] = jnp.concatenate(parts, axis=0).astype(BF16)

    def clear(where, first, count):
        @pl.when(jnp.logical_not(where))
        def _():
            kvext[:, first : first + count, :] = jnp.zeros((2, count, width), BF16)


    for g in range(groups):
        begin(row_detours(g))
        begin(row_copies(g))
    for g in range(groups):
        begin(frame_copies(g))
    loads[3].wait()
    for side in range(2):
        w_copy(1, side).start()
    clear(before_t, early, wing)
    clear(after_t, later, wing)
    clear(before_h, up, strip)
    clear(after_h, down, strip)
    for base in (early, later):
        clear(before_h, base + side_rows, corner)
        clear(after_h, base + side_rows + corner, corner)
    loads[2].wait()
    ogown[...] = og4[...].reshape(tokens, model)
    for g in range(2):
        og_across(g).start()
    piece = table_ref[:, 0:1]
    hit = jnp.ones_like(piece)
    for s, (df, dr) in enumerate(ORDER):
        a, b = t + df, h + dr
        inside = (a >= 0) & (a < nt) & (b >= 0) & (b < nh)
        here = jnp.where(inside, valid_ref[lax.rem(a + nt, nt), lax.rem(b + nh, nh)], 0)
        hit = jnp.where(piece == s + 1, here, hit)
    near = (table_ref[:, 1:2] <= reach_ref[t, 0, h]) & (table_ref[:, 2:3] <= reach_ref[t, 1, h])
    bias[...] = jnp.broadcast_to(
        jnp.where((piece == 0) | (near & (hit == 1)), 0.0, -1e30), bias.shape
    )

    loads[4].wait()
    q2[...] = in4[2].reshape(tokens, width)
    og2[0:tokens, :] = ogown[:, xcols]

    def rows_in(g):
        finish(row_detours(g))
        begin(row_passes(g))
        finish(row_copies(g))
        begin(corner_copies(g))

    rows_in(0)
    w_poll(0)
    rows_in(1)
    for g in range(2, groups):
        og_across(g).start()
    w_poll(1)

    def nt_dot(a, b):
        return lax.dot_general(a, b, (((1,), (1,)), ((), ())), preferred_element_type=F32)

    def tn_dot(a, b):
        return lax.dot_general(a, b, (((0,), (0,)), ((), ())), preferred_element_type=F32)

    def nn_dot(a, b):
        return lax.dot_general(a, b, (((1,), (0,)), ((), ())), preferred_element_type=F32)

    def head(g, j):
        return pl.ds(pl.multiple_of(g * gsize + j * HEAD_DIM, HEAD_DIM), HEAD_DIM)

    def mix_copy(g, kind):
        if kind == 0:
            return remote(
                mix.at[pl.ds(0, tokens), gcols(g)], mix.at[pl.ds(tokens, tokens), gcols(g)],
                mx_s.at[g], mx_r.at[g], across)
        first = (kind - 1) * tokens
        return remote(
            mix.at[pl.ds(first, tokens), gcols(g)],
            mix.at[pl.ds(2 * tokens + first, tokens), gcols(g)],
            mc_s.at[kind - 1, g], mc_r.at[kind - 1, g], partner)

    def forward(g):
        for j in range(gheads):
            cs = head(g, j)
            scores = nt_dot(kvext[0, :, cs], q2[:, cs]) * scale + bias[...]
            e = jnp.exp(scores - jnp.max(scores, axis=0, keepdims=True))
            p = e * (1.0 / jnp.sum(e, axis=0, keepdims=True))
            prob[g * gheads + j] = p
            mix[0:tokens, cs] = tn_dot(p.astype(BF16), kvext[1, :, cs]).astype(BF16)
        mix_copy(g, 0).start()
        mix_copy(g, 1).start()

    def dm_copy(i):
        cs = gcols(turn[i])
        return remote(dms.at[:, cs], dmr.at[:, cs], dm_s.at[i], dm_r.at[i], across)

    def project(i):
        cs = gcols(turn[i])
        both = nt_dot(og2[...], wfull[cs, :])
        dmx[:, cs] = both[:tokens]
        dms[:, cs] = both[tokens:].astype(BF16)
        dm_copy(i).start()

    def shares_in(first, last):
        for i in range(first, last):
            for side in range(2):
                w_share(i, side).wait()

    def forward_in(g):
        finish(frame_copies(g))
        finish(corner_copies(g))
        forward(g)

    def mix_in(g):
        mix_copy(g, 0).wait()
        mix_copy(g, 2).start()

    forward_in(0)
    rows_in(2)
    w_poll(2)
    forward_in(1)
    rows_in(3)
    w_poll(3)
    forward_in(2)
    forward_in(3)
    for g in range(groups):
        finish(row_passes(g))
    for g in range(groups):
        og_across(g).wait()
    ogc[0 : 2 * tokens, :] = og2[:, mine]
    og_core = remote(
        og2.at[:, other], ogc.at[pl.ds(2 * tokens, 2 * tokens), :],
        og_s.at[groups], og_r.at[groups], partner)
    og_core.start()
    shares_in(0, 4)
    project(0)
    w_poll(4)
    for g in range(groups):
        mix_in(g)
    og_core.wait()
    for g in range(groups):
        mix_copy(g, 1).wait()
        mix_copy(g, 2).wait()

    def weight(g):
        span = pl.ds(pl.multiple_of(g * gsize, 128), gsize)
        gpart[span, :] = tn_dot(mix[:, span], ogc[...])

    def gw_copy(j, side):
        return remote(
            gws.at[side, j], gwr.at[side, j], gw_s.at[side, j], gw_r.at[side, j],
            (right, left)[side])

    def gw_send(j, side):
        part = j % 2 if side == 0 else 1 - j % 2
        blk = at(pos + (1 - 2 * side) * (nh // 2 - (j + 1) // 2))
        total = gpart[pl.ds(pl.multiple_of(blk * share + part * cut, 16), cut), :]
        if j >= 2:
            total += gwr[side, j - 2].astype(F32)
        gws[side, j] = total.astype(BF16)
        gw_copy(j, side).start()

    def gw_poll(j):
        for side in range(2):
            gw_copy(j, side).wait()
            if j + 2 < slots:
                gw_send(j + 2, side)

    def attn(i, carry):
        cs = pl.ds(pl.multiple_of(i * 256, 256), 256)
        both = nn_dot(mix[0 : 2 * tokens, :], wfull[:, cs])
        attn2[:, pl.ds(pl.multiple_of(x * half + i * 256, 256), 256)] = both[:tokens].astype(BF16)
        asend[:, cs] = both[tokens:].astype(BF16)
        return carry

    def wing_copies(i):
        g = turn[i]
        return (
            (before_t, after_t, remote(
                gsend.at[:, pl.ds(0, wing), gcols(g)], grecv.at[0, :, :, gcols(g)],
                g1_s.at[0, i], g1_r.at[0, i], prev_t)),
            (after_t, before_t, remote(
                gsend.at[:, pl.ds(wing, wing), gcols(g)], grecv.at[1, :, :, gcols(g)],
                g1_s.at[1, i], g1_r.at[1, i], next_t)),
        )

    def attn_across(g):
        cols = pl.ds(pl.multiple_of(x * half + g * gsize, 128), gsize)
        return remote(asend.at[:, gcols(g)], attn2.at[:, cols], at_s.at[g], at_r.at[g], across)

    def backward(i):
        g = turn[i]
        dm_copy(i).wait()
        for j in range(gheads):
            cs = head(g, j)
            p = prob[g * gheads + j]
            dm = (dmx[:, cs] + dmr[:, cs].astype(F32)).astype(BF16)
            dp = nt_dot(kvext[1, :, cs], dm)
            inner = jnp.sum(p * dp, axis=0, keepdims=True)
            ds = (p * (dp - inner) * scale).astype(BF16)
            dq2[:, cs] = tn_dot(ds, kvext[0, :, cs]).astype(BF16)
            for n, grad in enumerate((nn_dot(ds, q2[:, cs]), nn_dot(p.astype(BF16), dm))):
                acc[n, :, cs] = grad[:tokens]
                gsend[n, 0:nwing, cs] = grad[tokens : tokens + nwing].astype(BF16)
                ud[n, :, cs] = grad[tokens + nwing :]
        begin(wing_copies(i))

    zfar = groups - 1 - h // 2
    weight(zfar)
    for side in range(2):
        gw_send(0, side)
    w_poll(5)

    def rest(i, carry):
        weight(lax.rem(zfar + 1 + i, groups))
        return carry

    lax.fori_loop(0, groups - 1, rest, 0)
    for side in range(2):
        gw_send(1, side)
    shares_in(4, 6)
    project(1)
    project(2)
    backward(0)
    w_poll(6)
    shares_in(6, 7)
    project(3)
    gw_poll(0)
    backward(1)
    lax.fori_loop(0, half // 256, attn, 0)
    attn_across(0).start()
    gw_poll(1)
    backward(2)
    attn_across(1).start()

    def strip_copies(g):
        return (
            (before_h & ~down_src, after_h, remote(
                gsend.at[:, pl.ds(nwing, strip), gcols(g)], rrecv.at[0, :, :, gcols(g)],
                g2_s.at[0, g], g2_r.at[0, g], prev_h)),
            (after_h & ~up_src, before_h, remote(
                gsend.at[:, pl.ds(nwing + strip, strip), gcols(g)], rrecv.at[1, :, :, gcols(g)],
                g2_s.at[1, g], g2_r.at[1, g], next_h)),
        )

    def strip_detours(g):
        return (
            (down_src, down_mid, remote(
                gsend.at[:, pl.ds(nwing, strip), gcols(g)], gpass.at[:, :, gcols(g)], gp_s.at[0, g], gp_r.at[0, g], next_h)),
            (up_src, up_mid, remote(
                gsend.at[:, pl.ds(nwing + strip, strip), gcols(g)], gpass.at[:, :, gcols(g)], gp_s.at[0, g], gp_r.at[0, g], prev_h)),
        )

    def strip_passes(g):
        return (
            (down_mid, False, remote(
                gpass.at[:, :, gcols(g)], rrecv.at[0, :, :, gcols(g)], gp_s.at[1, g], g2_r.at[0, g], prev2_h)),
            (up_mid, False, remote(
                gpass.at[:, :, gcols(g)], rrecv.at[1, :, :, gcols(g)], gp_s.at[1, g], g2_r.at[1, g], next2_h)),
        )

    def fold(i):
        g = turn[i]
        cs = gcols(g)
        finish(wing_copies(i))
        for s, (here, tok, edge) in enumerate(
            ((after_t, tokens - side_rows, strip - corner), (before_t, 0, 0))
        ):
            @pl.when(here)
            def _():
                for n in range(2):
                    y = grecv[s, n, :, cs].astype(F32)
                    acc[n, tok : tok + side_rows, cs] += y[:side_rows]
                    ud[n, edge : edge + corner, cs] += y[side_rows : side_rows + corner]
                    ud[n, strip + edge : strip + edge + corner, cs] += y[side_rows + corner :]

        for n in range(2):
            gsend[n, nwing:, cs] = ud[n, :, cs].astype(BF16)
        begin(strip_detours(g))
        begin(strip_copies(g))

    def strips_in(g):
        finish(strip_detours(g))
        begin(strip_passes(g))

    fold(0)
    gw_poll(2)
    backward(3)
    attn_across(2).start()
    attn_across(3).start()
    fold(1)
    fold(2)
    gw_poll(3)
    fold(3)
    dq_ref[...] = dq2[...].reshape(*tile, width)
    strips_in(0)
    strips_in(1)
    gw_poll(4)
    strips_in(2)
    strips_in(3)
    gw_poll(5)
    for g in range(groups):
        cs = slice(g * gsize, (g + 1) * gsize)
        finish(strip_copies(g))
        for s, (here, first) in enumerate(((after_h, rows - HALO), (before_h, 0))):
            @pl.when(here)
            def _():
                for i in range(2):
                    y = rrecv[s, i, :, cs].astype(F32)
                    for f in range(frames):
                        a = (f * rows + first) * columns
                        n = HALO * columns
                        acc[i, a : a + n, cs] += y[f * n : (f + 1) * n]

        for i, ref in enumerate((dk_ref, dv_ref)):
            ref[:, :, :, cs] = acc[i, :, cs].astype(BF16).reshape(*tile, gsize)
    for g in range(groups):
        finish(strip_passes(g))
    for g in range(groups):
        attn_across(g).wait()
    attn_ref[...] = attn2[...].reshape(*tile, model)
    gw_poll(6)
    for part in range(2):
        base = pl.multiple_of(h * share + part * cut, 16)
        gw_ref[part * cut : (part + 1) * cut, :] = (
            gpart[pl.ds(base, cut), :]
            + gwr[0, slots - 1 - part].astype(F32)
            + gwr[1, slots - 2 + part].astype(F32)
        )


def pass_on(*refs):
    n = len(refs) // 2
    copies = [pltpu.make_async_copy(refs[i], refs[n + i], refs[2 * n].at[i]) for i in range(n)]
    for copy in copies:
        copy.start()
    for copy in copies:
        copy.wait()


def paired(nt, nh, queries, key_tokens, value_tokens, out_weight, out_grad, window_reach, tile_valid):
    frames, rows, columns, width = queries.shape
    model = out_grad.shape[3]
    share = out_weight.shape[0]
    tokens = frames * rows * columns
    heads = width // HEAD_DIM
    halo = sum(piece_sizes(frames, rows, columns))
    strip = frames * HALO * columns
    wing = HALO * rows * columns + 2 * HALO * HALO * columns
    ext = tokens + halo
    table = np.ascontiguousarray(key_table(frames, rows, columns, ORDER).T)
    half, quarter, cut, slots = model // 2, model // 4, share // 2, nh - 1
    vmem = pl.BlockSpec(memory_space=pltpu.VMEM)
    smem = pl.BlockSpec(memory_space=pltpu.SMEM)
    hbm = pl.BlockSpec(memory_space=pl.ANY)
    dma = pltpu.SemaphoreType.DMA
    tile = (frames, rows, columns)
    shapes = (
        jax.ShapeDtypeStruct((*tile, model), BF16),
        jax.ShapeDtypeStruct((*tile, width), BF16),
        jax.ShapeDtypeStruct((*tile, width), BF16),
        jax.ShapeDtypeStruct((*tile, width), BF16),
        jax.ShapeDtypeStruct((share, quarter), F32),
    )
    results = pl.pallas_call(
        functools.partial(paired_kernel, (nt, nh, frames, rows, columns)),
        out_shape=[pltpu.VMEM(s.shape, s.dtype) for s in shapes],
        in_specs=[hbm, hbm, hbm, hbm, hbm, vmem, smem, smem],
        out_specs=[vmem] * 5,
        scratch_shapes=[
            pltpu.VMEM((3, *tile, width), BF16),
            pltpu.VMEM((*tile, model), BF16),
            pltpu.VMEM((tokens, width), BF16),
            pltpu.VMEM((tokens, width), BF16),
            pltpu.VMEM((2, ext, width), BF16),
            pltpu.VMEM((2, 2, strip, width), BF16),
            pltpu.VMEM((width, half), BF16),
            pltpu.VMEM((tokens, model), BF16),
            pltpu.VMEM((2 * tokens, half), BF16),
            pltpu.VMEM((4 * tokens, quarter), BF16),
            pltpu.VMEM((heads, ext, tokens), F32),
            pltpu.VMEM((4 * tokens, width), BF16),
            pltpu.VMEM((tokens, width), F32),
            pltpu.VMEM((tokens, width), BF16),
            pltpu.VMEM((tokens, width), BF16),
            pltpu.VMEM((tokens, model), BF16),
            pltpu.VMEM((tokens, half), BF16),
            pltpu.VMEM((2, tokens, width), F32),
            pltpu.VMEM((2, 2 * strip, width), F32),
            pltpu.VMEM((2, halo, width), BF16),
            pltpu.VMEM((2, 2, wing, width), BF16),
            pltpu.VMEM((2, 2, strip, width), BF16),
            pltpu.VMEM((2, strip, width), BF16),
            pltpu.VMEM((2, strip, width), BF16),
            pltpu.VMEM((width, quarter), F32),
            pltpu.VMEM((2, slots, cut, quarter), BF16),
            pltpu.VMEM((2, slots, cut, quarter), BF16),
            pltpu.VMEM((ext, tokens), F32),
            dma((5,)), dma((2, 4)), dma((1, 4)), dma((2, 4)), dma((1, 4)), dma((2, 4)), dma((2, 4)), dma((2, 4)), dma((2, 4)), dma((4, 4)), dma((4, 4)),
            dma((2, slots)), dma((2, slots)), dma((2, slots)), dma((2, slots)),
            dma((5,)), dma((5,)), dma((4,)), dma((4,)), dma((2, 4)), dma((2, 4)),
            dma((4,)), dma((4,)), dma((4,)), dma((4,)),
            dma((2, 4)), dma((2, 4)), dma((2, 4)), dma((2, 4)), dma((2, slots)), dma((2, slots)),
        ],
        compiler_params=pltpu.CompilerParams(
            collective_id=1, has_side_effects=True, vmem_limit_bytes=56 * 2**20
        ),
    )(
        queries, key_tokens, value_tokens, out_grad, out_weight, table,
        jnp.transpose(window_reach, (0, 2, 1)), tile_valid,
    )
    return pl.pallas_call(
        pass_on,
        out_shape=shapes,
        in_specs=[vmem] * 5,
        out_specs=[hbm] * 5,
        scratch_shapes=[dma((5,))],
    )(*[pltpu.with_memory_space_constraint(r, pltpu.VMEM) for r in results])


def solution(mesh):
    tile = P("tm", "height", None, None)
    nt, nh = mesh.shape["tm"], mesh.shape["height"]
    body = paired if (nt, nh) == (4, 8) else shards
    return jax.shard_map(
        functools.partial(body, nt, nh),
        mesh=mesh,
        in_specs=(tile, tile, tile, P("height", None), tile, P(), P()),
        out_specs=(tile, tile, tile, tile, P("height", "tm")),
        check_vma=False,
    )
```
